256 devices in a mesh: ctx: 128 (over z, y_lo, x, core), dp: 2 (over y_hi).
Axes of the slice: x: 4, y: 4 (y_hi: 2, y_lo: 2; y = y_hi * 2 + y_lo), z: 8, core: 2. Of those that a mesh axis runs over, the one named last changes fastest.
Arguments:
- queries: bfloat16 [2, 2, 128, 64, 4096], P('dp', None, 'ctx'), may hold values from -6 to 6
- keys: bfloat16 [2, 2, 128, 64, 512], P('dp', None, 'ctx'), may hold values from -3 to 3
- values: bfloat16 [2, 2, 128, 64, 512], P('dp', None, 'ctx'), may hold values from -6 to 6
- cotangent: bfloat16 [2, 2, 128, 64, 4096], P('dp', None, 'ctx'), may hold values from -6 to 6
- doc_start: int32 [2, 2, 128, 64], P('dp', None, 'ctx'), may hold values from 0 to 16383, as said below
- loss_mask: int32 [2, 2, 128, 64], P('dp', None, 'ctx'), may hold values from 0 to 1, as said below
- seeds: int32 [2], P('dp'), may hold values from 0 to 999999
Outputs:
- attn_out: bfloat16 [2, 2, 128, 64, 4096], P('dp', None, 'ctx')
- grad_q: bfloat16 [2, 2, 128, 64, 4096], P('dp', None, 'ctx')
- grad_k: float32 [2, 2, 128, 64, 512], P('dp', None, 'ctx')
- grad_v: float32 [2, 2, 128, 64, 512], P('dp', None, 'ctx')
The draws below stay inside these ranges and needn't reach their ends.
Inputs may be any that keep to these rules, and one draw needn't show every extreme that they name: `doc_start`: each entry is the position of the first token of its token's document; documents are runs of consecutive positions of at most 256 tokens, and the first document of each sequence has exactly that many. `loss_mask`: the token at position 0 of each sequence is counted.
All inputs are finite; a program needn't handle non-finite values.
Results may differ from the reference program's by a relative error of at most 0.038.
Values may be sent and summed in bfloat16 or wider, within the bound.
A program may use at most 64 MiB of HBM per device.

```python
import math
import jax
import jax.numpy as jnp
from jax import lax

QUERY_HEADS = 32
KEY_VALUE_HEADS = 4
HEAD_SIZE = 128
SPAN_TOKENS = 64
REACH_SPANS = 4
TOKENS = 16384
DOC_MAX = 256
N_CTX = 128
N_DP = 2


def fold_line(line):
    spans = line.reshape((2 * N_CTX, SPAN_TOKENS) + line.shape[1:])
    return jnp.stack([spans[:N_CTX], spans[N_CTX:][::-1]])


def layout_positions():
    single = fold_line(jnp.arange(TOKENS, dtype=jnp.int32))
    return jnp.stack([single] * N_DP)


def draw_queries(key, part):
    lattice_shape = (N_DP, 2, N_CTX, SPAN_TOKENS)
    random_key = jax.random.fold_in(key, 7)
    result_tuple = jnp.clip(jax.random.normal(random_key, lattice_shape + (QUERY_HEADS * HEAD_SIZE,)), -4.0, 4.0)
    return result_tuple.astype(jnp.float32).astype(jnp.bfloat16)


def draw_keys(key, part):
    lattice_shape = (N_DP, 2, N_CTX, SPAN_TOKENS)
    random_key = jax.random.fold_in(key, 9)
    result_tuple = jnp.clip(jax.random.normal(random_key, lattice_shape + (KEY_VALUE_HEADS * HEAD_SIZE,)), -3.0, 3.0)
    return result_tuple.astype(jnp.float32).astype(jnp.bfloat16)


def draw_doc_start(key, part):
    rows = []
    for batch_rows in range(N_DP):
        lengths = jax.random.randint(jax.random.fold_in(jax.random.fold_in(key, 13), batch_rows), (TOKENS,), 1, DOC_MAX + 1).astype(jnp.int32)
        lengths = lengths.at[0].set(DOC_MAX)
        ends = jnp.cumsum(lengths).astype(jnp.int32)
        starts = ends - lengths
        which = jnp.searchsorted(ends, jnp.arange(TOKENS, dtype=jnp.int32), side='right')
        rows.append(fold_line(starts[which]))
    return jnp.stack(rows).astype(jnp.int32)


def draw_loss_mask(key, part):
    positions = layout_positions()
    ramp = jnp.minimum(positions, TOKENS - 1 - positions)
    drawn = jax.random.randint(jax.random.fold_in(key, 17), positions.shape, 0, TOKENS)
    counted = (drawn < TOKENS // 16 + ramp * 7 // 4) | (positions == 0)
    return counted.astype(jnp.int32)


def shard_levels(stream_key, dims, pieces, low, largest):
    factor_of, own = 1.0, jax.random.fold_in(stream_key, 6)
    for dim, blocks in pieces:
        draws = jnp.exp(jax.random.uniform(jax.random.fold_in(own, dim), (blocks,), jnp.float32, low / len(pieces), largest / len(pieces)))
        factor_of = factor_of * jnp.repeat(draws, dims[dim] // blocks).reshape([-1 if axis == dim else 1 for axis in range(len(dims))])
    return factor_of


def scatter_about(rng, extent, scale, most, cuts=(), kind=jnp.bfloat16):
    gain = shard_levels(rng, extent, cuts, -0.22, 0.18) if cuts else 1.0
    values = jax.random.normal(rng, extent, jnp.float32) * scale * gain
    return jnp.minimum(jnp.maximum(values, -most), most).astype(kind)


def setup_inputs(seed: int = 0) -> dict:
    key_list = jax.random.split(jax.random.key(seed), 8)
    return {
        "queries": draw_queries(jax.random.fold_in(key_list[7], 71), 0),
        "keys": draw_keys(jax.random.fold_in(key_list[7], 71), 0),
        "values": scatter_about(key_list[2], (N_DP, 2, N_CTX, SPAN_TOKENS, KEY_VALUE_HEADS * HEAD_SIZE), 1.0, 6.0, ((0, 2), (2, 128))),
        "cotangent": scatter_about(key_list[3], (N_DP, 2, N_CTX, SPAN_TOKENS, QUERY_HEADS * HEAD_SIZE), 1.0, 6.0, ((0, 2), (2, 128))),
        "doc_start": draw_doc_start(jax.random.fold_in(key_list[7], 71), 0),
        "loss_mask": draw_loss_mask(jax.random.fold_in(key_list[7], 71), 0),
        "seeds": jax.random.randint(key_list[6], (N_DP,), 0, 1000000).astype(jnp.int32),
    }


masking_fill = -1e+30
keep_scale = 1024.0 / 922.0

def keep_table(seed_value, head_indices, query_pos, key_pos):
    mixed = seed_value * 1000003 + head_indices * 7919 + query_pos * 40503 + key_pos * 9973
    mixed = mixed ^ jnp.right_shift(mixed, 15)
    mixed = mixed * 73244475
    mixed = mixed ^ jnp.right_shift(mixed, 13)
    mixed = mixed * 1274126177
    mixed = mixed ^ jnp.right_shift(mixed, 16)
    return jnp.where(jnp.bitwise_and(mixed, 1023) >= 102, keep_scale, 0.0).astype(jnp.float32)

def rounded(value):
    return lax.optimization_barrier(value.astype(jnp.bfloat16)).astype(jnp.float32)

def target_line(array_half):
    return jnp.concatenate([array_half[0], array_half[1][::-1]], axis=0)

def from_line(line):
    return jnp.stack([line[:N_CTX], line[N_CTX:][::-1]])

def reference(queries, keys, values, cotangent, doc_start, loss_mask, seeds):
    query_groups = QUERY_HEADS // KEY_VALUE_HEADS
    span_window = (REACH_SPANS + 1) * SPAN_TOKENS
    inverse = 1.0 / math.sqrt(HEAD_SIZE)
    total_count = jnp.sum(loss_mask, dtype=jnp.int32)
    factor = N_DP * TOKENS / total_count.astype(jnp.float32)
    head_indices = jnp.arange(QUERY_HEADS, dtype=jnp.int32).reshape(KEY_VALUE_HEADS, query_groups, 1, 1)
    span_list = jnp.arange(2 * N_CTX, dtype=jnp.int32)
    result_out, result_dq, result_dk, result_dv = ([], [], [], [])
    for batch_rows in range(N_DP):
        query_row_line = target_line(queries[batch_rows])
        key_padding = jnp.concatenate([jnp.zeros((REACH_SPANS, SPAN_TOKENS, KEY_VALUE_HEADS * HEAD_SIZE), keys.dtype), target_line(keys[batch_rows])], axis=0)
        value_padding = jnp.concatenate([jnp.zeros((REACH_SPANS, SPAN_TOKENS, KEY_VALUE_HEADS * HEAD_SIZE), values.dtype), target_line(values[batch_rows])], axis=0)
        start_line = target_line(doc_start[batch_rows])
        weight_line = target_line(loss_mask[batch_rows]).astype(jnp.float32) * factor
        gradient_line = (target_line(cotangent[batch_rows]).astype(jnp.float32) * weight_line[:, :, None]).astype(jnp.bfloat16)
        seed_value = seeds[batch_rows]

        def block_parts(span_index):
            query_tile_block = query_row_line[span_index].reshape(SPAN_TOKENS, KEY_VALUE_HEADS, query_groups, HEAD_SIZE).astype(jnp.float32)
            key_tile_block = lax.dynamic_slice_in_dim(key_padding, span_index, REACH_SPANS + 1, 0).reshape(span_window, KEY_VALUE_HEADS, HEAD_SIZE)
            value_tile_block = lax.dynamic_slice_in_dim(value_padding, span_index, REACH_SPANS + 1, 0).reshape(span_window, KEY_VALUE_HEADS, HEAD_SIZE)
            query_pos = span_index * SPAN_TOKENS + jnp.arange(SPAN_TOKENS, dtype=jnp.int32)
            key_pos = (span_index - REACH_SPANS) * SPAN_TOKENS + jnp.arange(span_window, dtype=jnp.int32)
            starts_here = start_line[span_index]
            allowed = (key_pos[None, :] >= starts_here[:, None]) & (key_pos[None, :] <= query_pos[:, None])
            scores = jnp.einsum('qhgd,whd->hgqw', query_tile_block, key_tile_block.astype(jnp.float32)) * inverse
            dropkeep = keep_table(seed_value, head_indices, query_pos[:, None], key_pos[None, :])
            return (query_tile_block, key_tile_block.astype(jnp.float32), value_tile_block.astype(jnp.float32), allowed, scores, dropkeep)

        def forward_span(span_index):
            query_tile_block, key_tile_block, value_tile_block, allowed, scores, dropkeep = block_parts(span_index)
            top_score = lax.optimization_barrier(jnp.max(jnp.where(allowed, scores, masking_fill), axis=-1))
            expo = jnp.where(allowed, jnp.exp(scores - top_score[..., None]), 0.0)
            log_total = top_score + jnp.log(lax.optimization_barrier(jnp.sum(expo, axis=-1)))
            probs = jnp.where(allowed, jnp.exp(scores - log_total[..., None]), 0.0)
            dropped = rounded(probs * dropkeep)
            mixed_rows = jnp.einsum('hgqw,whd->qhgd', dropped, value_tile_block)
            return (mixed_rows.reshape(SPAN_TOKENS, QUERY_HEADS * HEAD_SIZE).astype(jnp.bfloat16), log_total)
        out_line, lse_line = lax.map(forward_span, span_list)
        inner_product = gradient_line.astype(jnp.float32) * out_line.astype(jnp.float32)
        delta_row_line = lax.optimization_barrier(jnp.sum(inner_product.reshape(2 * N_CTX, SPAN_TOKENS, KEY_VALUE_HEADS, query_groups, HEAD_SIZE), axis=-1)).transpose(0, 2, 3, 1)

        def backward_span(running, span_index):
            key_gradient_parts, value_gradient_parts = running
            query_tile_block, key_tile_block, value_tile_block, allowed, scores, dropkeep = block_parts(span_index)
            probs = jnp.where(allowed, jnp.exp(scores - lse_line[span_index][..., None]), 0.0)
            dropped = rounded(probs * dropkeep)
            gradient_block = gradient_line[span_index].reshape(SPAN_TOKENS, KEY_VALUE_HEADS, query_groups, HEAD_SIZE).astype(jnp.float32)
            value_gradient = jnp.einsum('hgqw,qhgd->whd', dropped, gradient_block)
            prob_grad = jnp.einsum('qhgd,whd->hgqw', gradient_block, value_tile_block)
            score_grad = rounded(probs * (prob_grad * dropkeep - delta_row_line[span_index][..., None]) * inverse)
            query_gradient = jnp.einsum('hgqw,whd->qhgd', score_grad, key_tile_block).reshape(SPAN_TOKENS, QUERY_HEADS * HEAD_SIZE).astype(jnp.bfloat16)
            key_gradient = jnp.einsum('hgqw,qhgd->whd', score_grad, query_tile_block)
            earlier_keys = lax.dynamic_slice_in_dim(key_gradient_parts, span_index, REACH_SPANS + 1, 0)
            earlier_values = lax.dynamic_slice_in_dim(value_gradient_parts, span_index, REACH_SPANS + 1, 0)
            key_gradient_parts = lax.dynamic_update_slice_in_dim(key_gradient_parts, earlier_keys + key_gradient.reshape(REACH_SPANS + 1, SPAN_TOKENS, KEY_VALUE_HEADS * HEAD_SIZE), span_index, 0)
            value_gradient_parts = lax.dynamic_update_slice_in_dim(value_gradient_parts, earlier_values + value_gradient.reshape(REACH_SPANS + 1, SPAN_TOKENS, KEY_VALUE_HEADS * HEAD_SIZE), span_index, 0)
            return ((key_gradient_parts, value_gradient_parts), query_gradient)
        empty_block = jnp.zeros((2 * N_CTX + REACH_SPANS, SPAN_TOKENS, KEY_VALUE_HEADS * HEAD_SIZE), jnp.float32)
        (key_gradient_parts, value_gradient_parts), dq_line = lax.scan(backward_span, (empty_block, empty_block), span_list)
        result_out.append(from_line(out_line))
        result_dq.append(from_line(dq_line))
        result_dk.append(from_line(key_gradient_parts[REACH_SPANS:]))
        result_dv.append(from_line(value_gradient_parts[REACH_SPANS:]))
    return (jnp.stack(result_out), jnp.stack(result_dq), jnp.stack(result_dk), jnp.stack(result_dv))
```

```python
import functools
import math

import jax
import jax.numpy as jnp
from jax import lax
from jax.experimental import pallas as pl
from jax.experimental.pallas import tpu as pltpu
from jax.sharding import PartitionSpec as P

SPAN = 64
GROUPS = 4
HEADS = 32
HEAD = 128
INV = 1.0 / math.sqrt(HEAD)
KEEP_SCALE = 1024.0 / 922.0
EXP2_SCALE = INV * math.log2(math.e)
MASKED = -1e30
MESH = pl.DeviceIdType.MESH


def nt(a, b):
    return lax.dot_general(a, b, (((1,), (1,)), ((), ())), preferred_element_type=jnp.float32)


def nn(a, b):
    return lax.dot_general(a, b, (((1,), (0,)), ((), ())), preferred_element_type=jnp.float32)


def keep_mask(mixed):
    mixed = mixed ^ lax.shift_right_arithmetic(mixed, 15)
    mixed = mixed * 73244475
    mixed = mixed ^ lax.shift_right_arithmetic(mixed, 13)
    mixed = mixed * 1274126177
    mixed = mixed ^ lax.shift_right_arithmetic(mixed, 16)
    return (mixed & 1023) >= 102


def relative_positions():
    row = lax.broadcasted_iota(jnp.int32, (256, 128), 0)
    offset = lax.broadcasted_iota(jnp.int32, (256, 128), 1) & 63
    tile = row >> 6
    inner = row & 63
    behind = jnp.where(tile == 3, jnp.where(inner <= offset, 0, 4), tile + 1)
    return inner - 64 * behind


def kernel(n, dims, q_hbm, do_hbm, k_hbm, v_hbm, start_ref, mask_ref, seed_ref,
           o_hbm, dq_hbm, dk_hbm, dv_hbm,
           q_ref, do_ref, o_ref, dq_ref, dqo_ref, dkv_ref,
           win, part, own, rx1, tot, rx2, rel_ref, mt_ref, pm_ref, ds_ref, acc, cbuf, fac_ref,
           in_sem, kv_sem, out_sem, kvout_sem,
           up_s, up_r, pt_s, pt_r, g1_s, g1_r, g2_s, g2_r, c_s, c_r):
    i = lax.axis_index("ctx")
    dp = lax.axis_index("dp")
    n_dp = lax.axis_size("dp")
    nz, ny, nx, nc = dims
    core = i % nc
    x = (i // nc) % nx
    ylo = (i // (nc * nx)) % ny
    z = i // (nc * nx * ny)
    partner = i + 1 - 2 * core
    spans = (i, 2 * n - 1 - i)
    rs = (core, 1 - core)

    def dev(c, d=dp):
        return {"ctx": c, "dp": d}

    def pdev(d):
        return jnp.where(i + d < n, i + d, 2 * n - 1 - i - d)

    def cidx(z_, y_, x_):
        return ((z_ * ny + y_) * nx + x_) * nc + core

    def count_peers(stage):
        peers = []
        if stage == 0:
            peers.append(dev(partner))
        elif stage == 1:
            for t in range(1, nx):
                peers.append(dev(cidx(z, ylo, (x + t) % nx)))
        elif stage == 2:
            both = dp * ny + ylo
            for t in range(1, ny * n_dp):
                other = (both + t) % (ny * n_dp)
                peers.append(dev(cidx(z, other % ny, x), other // ny))
        else:
            for t in range(1, nz):
                peers.append(dev(cidx((z + t) % nz, ylo, x)))
        return peers

    def count_copy(stage, t, target):
        return pltpu.make_async_remote_copy(
            acc.at[stage], cbuf.at[stage, t], c_s.at[stage, t], c_r.at[stage, t],
            device_id=target, device_id_type=MESH)

    def count_send(stage):
        for t, target in enumerate(count_peers(stage)):
            count_copy(stage, t, target).start()

    def count_take(stage):
        total = acc[stage]
        for t, target in enumerate(count_peers(stage)):
            cp = count_copy(stage, t, target)
            cp.wait_recv()
            cp.wait_send()
            total = total + cbuf[stage, t]
        acc[stage + 1] = total

    ins = []
    for h in range(2):
        for g in range(GROUPS):
            for w, src in enumerate((k_hbm, v_hbm)):
                cp = pltpu.make_async_copy(src.at[h, :, pl.ds(g * 128, 128)], win.at[g, h, 0, w], kv_sem.at[g, h, w])
                cp.start()
                ins.append(cp)
    cq = pltpu.make_async_copy(q_hbm, q_ref, in_sem.at[0])
    cd = pltpu.make_async_copy(do_hbm, do_ref, in_sem.at[1])
    cq.start()
    cd.start()

    barrier = pltpu.get_barrier_semaphore()

    def greet(target):
        pl.semaphore_signal(barrier, inc=1, device_id=target, device_id_type=MESH)

    n_greet = 0
    for d in (2, 4):
        greet(dev(pdev(d)))
        n_greet += 1
        pl.when(i >= d)(lambda d=d: greet(dev(i - d)))
    for stage in range(4):
        for target in count_peers(stage):
            greet(target)
            n_greet += 1

    rel_ref[...] = relative_positions()
    mask = mask_ref[...]
    acc[0] = jnp.pad(mask[0:1] + mask[1:2], ((0, 7), (0, 64)))
    for h in range(2):
        m = mask[h:h + 1].astype(jnp.float32)
        m2 = jnp.concatenate([m, m], axis=1)
        mt_ref[h] = jnp.broadcast_to(m2, (128, 128)).T.astype(jnp.bfloat16)
    for d in (2, 4):
        @pl.when(i < d)
        def _():
            win[:, 0, d] = jnp.zeros((GROUPS, 2, SPAN, HEAD), jnp.bfloat16)
            rx2[:, 1, d // 2 - 1] = jnp.zeros((GROUPS, 2, SPAN, HEAD), jnp.bfloat16)

    pl.semaphore_wait(barrier, n_greet + (i >= 2).astype(jnp.int32) + (i >= 4).astype(jnp.int32))

    def up_copy(g, h, d):
        e = d // 2 - 1
        if h == 0:
            half, target = jnp.where(i + d < n, 0, 1), dev(pdev(d))
        else:
            half, target = 1, dev(i - d)
        return pltpu.make_async_remote_copy(
            win.at[g, h, 0], win.at[g, half, d], up_s.at[g, h, e], up_r.at[g, half, e],
            device_id=target, device_id_type=MESH)

    def up_arrived(g, h, d):
        e = d // 2 - 1
        pltpu.make_async_remote_copy(
            win.at[g, h, d], win.at[g, h, d], up_s.at[g, h, e], up_r.at[g, h, e],
            device_id=dev(partner), device_id_type=MESH).wait_recv()

    def partner_copy(g, h, e):
        slot = 2 * rs[h] + 2 * e
        return pltpu.make_async_remote_copy(
            win.at[g, h, slot], win.at[g, h, 1 + 2 * e], pt_s.at[g, h, e], pt_r.at[g, h, e],
            device_id=dev(partner), device_id_type=MESH)

    for cp in ins:
        cp.wait()
    for g in range(GROUPS):
        for d in (4, 2):
            up_copy(g, 0, d).start()

            @pl.when(i >= d)
            def _():
                up_copy(g, 1, d).start()
    count_send(0)

    def relay(g):
        for d in (2, 4):
            pl.when(i >= d)(lambda d=d: up_arrived(g, 0, d))
            up_arrived(g, 1, d)
        for h in range(2):
            for e in range(2):
                partner_copy(g, h, e).start()

    count_take(0)
    count_send(1)
    cq.wait()
    cd.wait()
    relay(0)
    count_take(1)
    count_send(2)

    lane = lax.broadcasted_iota(jnp.int32, (1, 128), 1)
    tri = lax.broadcasted_iota(jnp.int32, (64, 128), 0) <= (lane & 63)

    def grad1_copy(g, h, e):
        return pltpu.make_async_remote_copy(
            part.at[g, h, 1 + 2 * e], rx1.at[g, h, e], g1_s.at[g, h, e], g1_r.at[g, h, e],
            device_id=dev(partner), device_id_type=MESH)

    def grad2_copy(g, h, d):
        e = d // 2 - 1
        if h == 0:
            half, target = 0, dev(i - d)
        else:
            half, target = jnp.where(i + d < n, 1, 0), dev(pdev(d))
        return pltpu.make_async_remote_copy(
            tot.at[g, h, e], rx2.at[g, half, e], g2_s.at[g, h, e], g2_r.at[g, half, e],
            device_id=target, device_id_type=MESH)

    def compute(g, h):
        span = spans[h]
        for e in range(2):
            partner_copy(g, h, e).wait_recv()
        kw = win[g, h, :, 0].reshape(320, 128)
        vw = win[g, h, :, 1].reshape(320, 128)
        kt = kw.T
        vt = vw.T
        start_row = start_ref[h:h + 1]
        start2 = jnp.concatenate([start_row, start_row], axis=1) - span * SPAN
        base = seed_ref[0] * 1000003 + span * SPAN * 9973
        mt = mt_ref[h, 0:64]
        col0 = (span * SPAN + (lane & 63)) * 40503 + base + (lane >> 6) * 7919

        def head_cols(j):
            return pl.ds(pl.multiple_of(g * 1024 + j * 128, 128), 128)

        for hh in range(2):
            q4 = jnp.concatenate([q_ref[h, :, head_cols(hh * 4 + j)] for j in range(4)], axis=0)
            d4 = jnp.concatenate([do_ref[h, :, head_cols(hh * 4 + j)] * mt for j in range(4)], axis=0)
            s4 = nt(kw, q4)
            g4 = nt(vw, d4)
            for pr in range(2):
                cs = slice(pr * 128, pr * 128 + 128)
                rel = rel_ref[...]
                keep = keep_mask(rel * 9973 + (col0 + (g * 8 + hh * 4 + pr * 2) * 7919))
                s = jnp.concatenate([s4[64:256, cs], jnp.where(tri, s4[:64, cs], s4[256:, cs])], axis=0)
                s = jnp.where(rel >= start2, s, MASKED)
                top = jnp.max(s, axis=0, keepdims=True)
                e = jnp.exp2((s - top) * EXP2_SCALE)
                p = e * (1.0 / jnp.sum(e, axis=0, keepdims=True))
                dp_ = jnp.concatenate([g4[64:256, cs], jnp.where(tri, g4[:64, cs], g4[256:, cs])], axis=0)
                gk = jnp.where(keep, dp_, 0.0)
                delta = jnp.sum(p * gk, axis=0, keepdims=True)
                ds = p * (gk - delta)
                pm = jnp.where(keep, p, 0.0)
                oc = slice(hh * 256 + pr * 128, hh * 256 + pr * 128 + 128)
                for ref, val in ((pm_ref, pm), (ds_ref, ds)):
                    ref[0:64, oc] = jnp.where(tri, val[192:], 0.0).astype(jnp.bfloat16)
                    ref[64:256, oc] = val[:192].astype(jnp.bfloat16)
                    ref[256:320, oc] = jnp.where(tri, 0.0, val[192:]).astype(jnp.bfloat16)
            ot = nn(vt, pm_ref[:, hh * 256:hh * 256 + 256]) * KEEP_SCALE
            dqt = nn(kt, ds_ref[:, hh * 256:hh * 256 + 256])
            oo = ot.T.astype(jnp.bfloat16)
            dq = dqt.T
            for j in range(4):
                o_ref[h, :, head_cols(hh * 4 + j)] = oo[j * 64:(j + 1) * 64]
                dq_ref[h, :, head_cols(hh * 4 + j)] = dq[j * 64:(j + 1) * 64]
        qall = jnp.concatenate([q_ref[h, :, head_cols(j)] for j in range(8)], axis=0)
        dall = jnp.concatenate([do_ref[h, :, head_cols(j)] * mt for j in range(8)], axis=0)
        dv = nn(pm_ref[...], dall)
        dk = nn(ds_ref[...], qall) * INV
        own[g, h, 0] = dk[0:64]
        own[g, h, 1] = dv[0:64]
        part[g, h, :, 0] = dk.reshape(5, SPAN, HEAD).astype(jnp.bfloat16)
        part[g, h, :, 1] = dv.reshape(5, SPAN, HEAD).astype(jnp.bfloat16)
        for e in range(2):
            grad1_copy(g, h, e).start()

    def combine(g, h):
        r = rs[h]
        rf = r.astype(jnp.float32)
        for e in range(2):
            grad1_copy(g, h, e).wait_recv()
        x1 = rx1[g, h, 0].astype(jnp.float32)
        x3 = rx1[g, h, 1].astype(jnp.float32)
        own[g, h] = own[g, h] + (1.0 - rf) * x1
        tot[g, h, 0] = (part[g, h, 2].astype(jnp.float32) + rf * x1 + (1.0 - rf) * x3).astype(jnp.bfloat16)
        tot[g, h, 1] = (part[g, h, 4].astype(jnp.float32) + rf * x3).astype(jnp.bfloat16)
        for d in (2, 4):
            if h == 0:
                pl.when(i >= d)(lambda d=d: grad2_copy(g, h, d).start())
            else:
                grad2_copy(g, h, d).start()

    def out_copy(which, g):
        src, dst = ((o_ref, o_hbm), (dqo_ref, dq_hbm))[which]
        cols = pl.ds(pl.multiple_of(g * 1024, 1024), 1024)
        return pltpu.make_async_copy(src.at[:, :, cols], dst.at[:, :, cols], out_sem.at[which, g])

    def finalize(g):
        cols = pl.ds(pl.multiple_of(g * 1024, 1024), 1024)
        scale = fac_ref[0:1, 0:1] * (KEEP_SCALE * INV)
        dqo_ref[:, :, cols] = (dq_ref[:, :, cols] * scale).astype(jnp.bfloat16)
        out_copy(1, g).start()

    count_take(2)
    count_send(3)

    def step(g, carry):
        compute(g, 0)

        @pl.when(g > 0)
        def _():
            combine(g - 1, 1)

        @pl.when(g < GROUPS - 1)
        def _():
            relay(g + 1)

        @pl.when(g == 1)
        def _():
            count_take(3)
            total = jnp.sum(acc[4].astype(jnp.float32))
            slots = float(2 * 2 * n * SPAN)
            fac_ref[...] = jnp.full((8, 128), slots, jnp.float32) / jnp.full((8, 128), total, jnp.float32)

        @pl.when(g > 0)
        def _():
            finalize(g - 1)

        compute(g, 1)
        combine(g, 0)
        out_copy(0, g).start()
        return carry

    lax.fori_loop(0, GROUPS, step, 0)
    combine(GROUPS - 1, 1)
    finalize(GROUPS - 1)

    def final(g, carry):
        for h in range(2):
            for d in (2, 4):
                def arrived(d=d):
                    e = d // 2 - 1
                    pltpu.make_async_remote_copy(
                        tot.at[g, h, e], rx2.at[g, h, e], g2_s.at[g, h, e], g2_r.at[g, h, e],
                        device_id=dev(partner), device_id_type=MESH).wait_recv()
                if h == 0:
                    arrived()
                else:
                    pl.when(i >= d)(arrived)
            scale = fac_ref[0:1, 0:1] * KEEP_SCALE
            val = (own[g, h] + rx2[g, h, 0].astype(jnp.float32) + rx2[g, h, 1].astype(jnp.float32)) * scale
            cols = pl.ds(pl.multiple_of(g * 128, 128), 128)
            dkv_ref[0, h, :, cols] = val[0]
            dkv_ref[1, h, :, cols] = val[1]
        return carry

    lax.fori_loop(0, GROUPS, final, 0)
    ck = pltpu.make_async_copy(dkv_ref.at[0], dk_hbm, kvout_sem.at[0])
    cv = pltpu.make_async_copy(dkv_ref.at[1], dv_hbm, kvout_sem.at[1])
    ck.start()
    cv.start()

    def drain(g, carry):
        for h in range(2):
            for e in range(2):
                d = 2 * e + 2
                partner_copy(g, h, e).wait_send()
                grad1_copy(g, h, e).wait_send()
                if h == 0:
                    up_copy(g, h, d).wait_send()
                    pl.when(i >= d)(lambda d=d: grad2_copy(g, 0, d).wait_send())
                else:
                    pl.when(i >= d)(lambda d=d: up_copy(g, 1, d).wait_send())
                    grad2_copy(g, h, d).wait_send()
        out_copy(0, g).wait()
        out_copy(1, g).wait()
        return carry

    lax.fori_loop(0, GROUPS, drain, 0)
    ck.wait()
    cv.wait()


def grid_of(n):
    nc, nx = 2, 4
    ny = 2 if n // (nc * nx) > 1 else 1
    return (n // (nc * nx * ny), ny, nx, nc)


def body(queries, keys, values, cotangent, doc_start, loss_mask, seeds):
    n = lax.axis_size("ctx")
    dims = grid_of(n)
    peers = max(1, dims[2] - 1, dims[1] * lax.axis_size("dp") - 1, dims[0] - 1)
    wide = (2, SPAN, HEADS * HEAD)
    narrow = (2, SPAN, GROUPS * HEAD)
    bf16, f32, i32 = jnp.bfloat16, jnp.float32, jnp.int32
    hbm = pl.BlockSpec(memory_space=pl.ANY)
    vmem = pl.BlockSpec(memory_space=pltpu.VMEM)
    dma = pltpu.SemaphoreType.DMA
    pair = (2, SPAN, HEAD)
    outs = pl.pallas_call(
        functools.partial(kernel, n, dims),
        out_shape=[
            jax.ShapeDtypeStruct(wide, bf16),
            jax.ShapeDtypeStruct(wide, bf16),
            jax.ShapeDtypeStruct(narrow, f32),
            jax.ShapeDtypeStruct(narrow, f32),
        ],
        in_specs=[hbm] * 4 + [vmem, vmem, pl.BlockSpec(memory_space=pltpu.SMEM)],
        out_specs=[hbm] * 4,
        scratch_shapes=[
            pltpu.VMEM(wide, bf16),
            pltpu.VMEM(wide, bf16),
            pltpu.VMEM(wide, bf16),
            pltpu.VMEM(wide, f32),
            pltpu.VMEM(wide, bf16),
            pltpu.VMEM((2,) + narrow, f32),
            pltpu.VMEM((GROUPS, 2, 5) + pair, bf16),
            pltpu.VMEM((GROUPS, 2, 5) + pair, bf16),
            pltpu.VMEM((GROUPS, 2) + pair, f32),
            pltpu.VMEM((GROUPS, 2, 2) + pair, bf16),
            pltpu.VMEM((GROUPS, 2, 2) + pair, bf16),
            pltpu.VMEM((GROUPS, 2, 2) + pair, bf16),
            pltpu.VMEM((256, 128), i32),
            pltpu.VMEM((2, 128, 128), bf16),
            pltpu.VMEM((320, 512), bf16),
            pltpu.VMEM((320, 512), bf16),
            pltpu.VMEM((5, 8, 128), i32),
            pltpu.VMEM((4, peers, 8, 128), i32),
            pltpu.VMEM((8, 128), f32),
            dma((2,)),
            dma((GROUPS, 2, 2)),
            dma((2, GROUPS)),
            dma((2,)),
        ] + [dma((GROUPS, 2, 2))] * 8 + [dma((4, peers))] * 2,
        compiler_params=pltpu.CompilerParams(collective_id=0, has_side_effects=True),
        name="attention",
    )(
        queries.reshape(wide),
        cotangent.reshape(wide),
        keys.reshape(narrow),
        values.reshape(narrow),
        doc_start.reshape(2, SPAN),
        loss_mask.reshape(2, SPAN),
        seeds,
    )
    return (
        outs[0].reshape(queries.shape),
        outs[1].reshape(queries.shape),
        outs[2].reshape(keys.shape),
        outs[3].reshape(values.shape),
    )


def solution(mesh):
    wide = P("dp", None, "ctx", None, None)
    flat = P("dp", None, "ctx", None)
    return jax.shard_map(
        body,
        mesh=mesh,
        in_specs=(wide, wide, wide, wide, flat, flat, P("dp")),
        out_specs=(wide, wide, wide, wide),
        check_vma=False,
    )
```

```python
import functools
import math

import jax
import jax.numpy as jnp
from jax import lax
from jax.experimental import pallas as pl
from jax.experimental.pallas import tpu as pltpu
from jax.sharding import PartitionSpec as P

SPAN = 64
GROUPS = 4
HEADS = 32
HEAD = 128
INV = 1.0 / math.sqrt(HEAD)
KEEP_SCALE = 1024.0 / 922.0
EXP2_SCALE = INV * math.log2(math.e)
MASKED = -1e30
MESH = pl.DeviceIdType.MESH


def nt(a, b):
    return lax.dot_general(a, b, (((1,), (1,)), ((), ())), preferred_element_type=jnp.float32)


def nn(a, b):
    return lax.dot_general(a, b, (((1,), (0,)), ((), ())), preferred_element_type=jnp.float32)


def keep_mask(mixed):
    mixed = mixed ^ lax.shift_right_arithmetic(mixed, 15)
    mixed = mixed * 73244475
    mixed = mixed ^ lax.shift_right_arithmetic(mixed, 13)
    mixed = mixed * 1274126177
    mixed = mixed ^ lax.shift_right_arithmetic(mixed, 16)
    return (mixed & 1023) >= 102


def relative_positions():
    row = lax.broadcasted_iota(jnp.int32, (256, 128), 0)
    offset = lax.broadcasted_iota(jnp.int32, (256, 128), 1) & 63
    tile = row >> 6
    inner = row & 63
    behind = jnp.where(tile == 3, jnp.where(inner <= offset, 0, 4), tile + 1)
    return inner - 64 * behind


def kernel(n, dims, q_hbm, do_hbm, k_hbm, v_hbm, start_ref, mask_ref, seed_ref,
           o_ref, dqo_ref, dkv_ref,
           q_ref, do_ref, dq_ref,
           win, part, own, rx1, tot, rx2, keep_ref, bias_ref, mt_ref, pm_ref, ds_ref, acc, cbuf, fac_ref,
           in_sem, kv_sem,
           up_s, up_r, pt_s, pt_r, g1_s, g1_r, g2_s, g2_r, c_s, c_r):
    i = lax.axis_index("ctx")
    dp = lax.axis_index("dp")
    n_dp = lax.axis_size("dp")
    nz, ny, nx, nc = dims
    core = i % nc
    x = (i // nc) % nx
    ylo = (i // (nc * nx)) % ny
    z = i // (nc * nx * ny)
    partner = i + 1 - 2 * core
    spans = (i, 2 * n - 1 - i)
    rs = (core, 1 - core)

    def dev(c, d=dp):
        return {"ctx": c, "dp": d}

    def pdev(d):
        return jnp.where(i + d < n, i + d, 2 * n - 1 - i - d)

    def cidx(z_, y_, x_):
        return ((z_ * ny + y_) * nx + x_) * nc + core

    def count_peers(stage):
        peers = []
        if stage == 0:
            peers.append(dev(partner))
        elif stage == 1:
            for t in range(1, nx):
                peers.append(dev(cidx(z, ylo, (x + t) % nx)))
        elif stage == 2:
            both = dp * ny + ylo
            for t in range(1, ny * n_dp):
                other = (both + t) % (ny * n_dp)
                peers.append(dev(cidx(z, other % ny, x), other // ny))
        else:
            for t in range(1, nz):
                peers.append(dev(cidx((z + t) % nz, ylo, x)))
        return peers

    def count_copy(stage, t, target):
        return pltpu.make_async_remote_copy(
            acc.at[stage], cbuf.at[stage, t], c_s.at[stage, t], c_r.at[stage, t],
            device_id=target, device_id_type=MESH)

    def count_send(stage):
        for t, target in enumerate(count_peers(stage)):
            count_copy(stage, t, target).start()

    def count_take(stage):
        total = acc[stage]
        for t, target in enumerate(count_peers(stage)):
            cp = count_copy(stage, t, target)
            cp.wait_recv()
            cp.wait_send()
            total = total + cbuf[stage, t]
        acc[stage + 1] = total

    ins = []
    for h in range(2):
        for g in range(GROUPS):
            for w, src in enumerate((k_hbm, v_hbm)):
                cp = pltpu.make_async_copy(src.at[h, :, pl.ds(g * 128, 128)], win.at[g, h, 0, w], kv_sem.at[g, h, w])
                cp.start()
                ins.append(cp)
    cq = pltpu.make_async_copy(q_hbm, q_ref, in_sem.at[0])
    cd = pltpu.make_async_copy(do_hbm, do_ref, in_sem.at[1])
    cq.start()
    cd.start()

    barrier = pltpu.get_barrier_semaphore()

    def greet(target):
        pl.semaphore_signal(barrier, inc=1, device_id=target, device_id_type=MESH)

    n_greet = 0
    for d in (2, 4):
        greet(dev(pdev(d)))
        n_greet += 1
        pl.when(i >= d)(lambda d=d: greet(dev(i - d)))
    for stage in range(4):
        for target in count_peers(stage):
            greet(target)
            n_greet += 1

    rel = relative_positions()
    mask = mask_ref[...]
    acc[0] = jnp.pad(mask[0:1] + mask[1:2], ((0, 7), (0, 64)))
    for h in range(2):
        m = mask[h:h + 1].astype(jnp.float32)
        m2 = jnp.concatenate([m, m], axis=1)
        mt_ref[h] = jnp.broadcast_to(m2, (128, 128)).T.astype(jnp.bfloat16)
        start_row = start_ref[h:h + 1]
        start2 = jnp.concatenate([start_row, start_row], axis=1) - spans[h] * SPAN
        bias_ref[h] = jnp.where(rel >= start2, 0.0, MASKED)
    for d in (2, 4):
        @pl.when(i < d)
        def _():
            win[:, 0, d] = jnp.zeros((GROUPS, 2, SPAN, HEAD), jnp.bfloat16)
            rx2[:, 1, d // 2 - 1] = jnp.zeros((GROUPS, 2, SPAN, HEAD), jnp.bfloat16)

    pl.semaphore_wait(barrier, n_greet + (i >= 2).astype(jnp.int32) + (i >= 4).astype(jnp.int32))

    def up_copy(g, h, d):
        e = d // 2 - 1
        if h == 0:
            half, target = jnp.where(i + d < n, 0, 1), dev(pdev(d))
        else:
            half, target = 1, dev(i - d)
        return pltpu.make_async_remote_copy(
            win.at[g, h, 0], win.at[g, half, d], up_s.at[g, h, e], up_r.at[g, half, e],
            device_id=target, device_id_type=MESH)

    def up_arrived(g, h, d):
        e = d // 2 - 1
        pltpu.make_async_remote_copy(
            win.at[g, h, d], win.at[g, h, d], up_s.at[g, h, e], up_r.at[g, h, e],
            device_id=dev(partner), device_id_type=MESH).wait_recv()

    def partner_copy(g, h, e):
        slot = 2 * rs[h] + 2 * e
        return pltpu.make_async_remote_copy(
            win.at[g, h, slot], win.at[g, h, 1 + 2 * e], pt_s.at[g, h, e], pt_r.at[g, h, e],
            device_id=dev(partner), device_id_type=MESH)

    for cp in ins:
        cp.wait()
    for g in range(GROUPS):
        for d in (4, 2):
            up_copy(g, 0, d).start()

            @pl.when(i >= d)
            def _():
                up_copy(g, 1, d).start()
    count_send(0)

    def relay(g):
        for d in (2, 4):
            pl.when(i >= d)(lambda d=d: up_arrived(g, 0, d))
            up_arrived(g, 1, d)
        for h in range(2):
            for e in range(2):
                partner_copy(g, h, e).start()

    lane = lax.broadcasted_iota(jnp.int32, (1, 128), 1)
    tri = lax.broadcasted_iota(jnp.int32, (64, 128), 0) <= (lane & 63)

    hashed = relative_positions() * 9973
    for h in range(2):
        base = seed_ref[0] * 1000003 + spans[h] * (SPAN * 9973)
        col0 = (spans[h] * SPAN + (lane & 63)) * 40503 + base + (lane >> 6) * 7919

        def fill(pair, carry, h=h, col0=col0):
            keep = keep_mask(hashed + (col0 + pair * (2 * 7919)))
            keep_ref[h, pair] = jnp.where(keep, 1.0, 0.0)
            return carry

        lax.fori_loop(0, HEADS // 2, fill, 0)

    cq.wait()
    cd.wait()
    relay(0)
    count_take(0)
    count_send(1)

    def grad1_copy(g, h, e):
        return pltpu.make_async_remote_copy(
            part.at[g, h, 1 + 2 * e], rx1.at[g, h, e], g1_s.at[g, h, e], g1_r.at[g, h, e],
            device_id=dev(partner), device_id_type=MESH)

    def grad2_copy(g, h, d):
        e = d // 2 - 1
        if h == 0:
            half, target = 0, dev(i - d)
        else:
            half, target = jnp.where(i + d < n, 1, 0), dev(pdev(d))
        return pltpu.make_async_remote_copy(
            tot.at[g, h, e], rx2.at[g, half, e], g2_s.at[g, h, e], g2_r.at[g, half, e],
            device_id=target, device_id_type=MESH)

    def compute(g, h):
        for e in range(2):
            partner_copy(g, h, e).wait_recv()
        kw = win[g, h, :, 0].reshape(320, 128)
        vw = win[g, h, :, 1].reshape(320, 128)
        kt = kw.T
        vt = vw.T
        mt = mt_ref[h, 0:64]

        def head_cols(j):
            return pl.ds(pl.multiple_of(g * 1024 + j * 128, 128), 128)

        for hh in range(2):
            q4 = jnp.concatenate([q_ref[h, :, head_cols(hh * 4 + j)] for j in range(4)], axis=0)
            d4 = jnp.concatenate([do_ref[h, :, head_cols(hh * 4 + j)] * mt for j in range(4)], axis=0)
            s4 = nt(kw, q4)
            g4 = nt(vw, d4)
            for pr in range(2):
                cs = slice(pr * 128, pr * 128 + 128)
                s = jnp.concatenate([s4[64:256, cs], jnp.where(tri, s4[:64, cs], s4[256:, cs])], axis=0)
                s = s + bias_ref[h]
                top = jnp.max(s, axis=0, keepdims=True)
                e = jnp.exp2((s - top) * EXP2_SCALE)
                p = e * (1.0 / jnp.sum(e, axis=0, keepdims=True))
                pm = p * keep_ref[h, g * 4 + hh * 2 + pr]
                dp_ = jnp.concatenate([g4[64:256, cs], jnp.where(tri, g4[:64, cs], g4[256:, cs])], axis=0)
                t = pm * dp_
                delta = jnp.sum(t, axis=0, keepdims=True)
                ds = t - p * delta
                oc = slice(hh * 256 + pr * 128, hh * 256 + pr * 128 + 128)
                for ref, val in ((pm_ref, pm), (ds_ref, ds)):
                    ref[0:64, oc] = jnp.where(tri, val[192:], 0.0).astype(jnp.bfloat16)
                    ref[64:256, oc] = val[:192].astype(jnp.bfloat16)
                    ref[256:320, oc] = jnp.where(tri, 0.0, val[192:]).astype(jnp.bfloat16)
            ot = nn(vt, pm_ref[:, hh * 256:hh * 256 + 256]) * KEEP_SCALE
            dqt = nn(kt, ds_ref[:, hh * 256:hh * 256 + 256])
            oo = ot.T.astype(jnp.bfloat16)
            dq = dqt.T
            for j in range(4):
                o_ref[h, :, head_cols(hh * 4 + j)] = oo[j * 64:(j + 1) * 64]
                dq_ref[h, :, head_cols(hh * 4 + j)] = dq[j * 64:(j + 1) * 64]
        qall = jnp.concatenate([q_ref[h, :, head_cols(j)] for j in range(8)], axis=0)
        dall = jnp.concatenate([do_ref[h, :, head_cols(j)] * mt for j in range(8)], axis=0)
        dv = nn(pm_ref[...], dall)
        dk = nn(ds_ref[...], qall) * INV
        own[g, h, 0] = dk[0:64]
        own[g, h, 1] = dv[0:64]
        part[g, h, :, 0] = dk.reshape(5, SPAN, HEAD).astype(jnp.bfloat16)
        part[g, h, :, 1] = dv.reshape(5, SPAN, HEAD).astype(jnp.bfloat16)
        for e in range(2):
            grad1_copy(g, h, e).start()

    def combine(g, h):
        r = rs[h]
        rf = r.astype(jnp.float32)
        for e in range(2):
            grad1_copy(g, h, e).wait_recv()
        x1 = rx1[g, h, 0].astype(jnp.float32)
        x3 = rx1[g, h, 1].astype(jnp.float32)
        own[g, h] = own[g, h] + (1.0 - rf) * x1
        tot[g, h, 0] = (part[g, h, 2].astype(jnp.float32) + rf * x1 + (1.0 - rf) * x3).astype(jnp.bfloat16)
        tot[g, h, 1] = (part[g, h, 4].astype(jnp.float32) + rf * x3).astype(jnp.bfloat16)
        for d in (2, 4):
            if h == 0:
                pl.when(i >= d)(lambda d=d: grad2_copy(g, h, d).start())
            else:
                grad2_copy(g, h, d).start()

    def finalize(g):
        cols = pl.ds(pl.multiple_of(g * 1024, 1024), 1024)
        scale = fac_ref[0:1, 0:1] * (KEEP_SCALE * INV)
        dqo_ref[:, :, cols] = (dq_ref[:, :, cols] * scale).astype(jnp.bfloat16)

    def step(g, carry):
        compute(g, 0)

        @pl.when(g > 0)
        def _():
            combine(g - 1, 1)

        @pl.when(g < GROUPS - 1)
        def _():
            relay(g + 1)

        compute(g, 1)
        combine(g, 0)

        @pl.when(g == 0)
        def _():
            count_take(1)
            count_send(2)

        @pl.when(g == 1)
        def _():
            count_take(2)
            count_send(3)

        return carry

    lax.fori_loop(0, GROUPS, step, 0)
    combine(GROUPS - 1, 1)
    count_take(3)
    total = jnp.sum(acc[4].astype(jnp.float32))
    slots = float(2 * 2 * n * SPAN)
    fac_ref[...] = jnp.full((8, 128), slots, jnp.float32) / jnp.full((8, 128), total, jnp.float32)
    for g in range(GROUPS):
        finalize(g)

    def final(g, carry):
        for h in range(2):
            for d in (2, 4):
                def arrived(d=d):
                    e = d // 2 - 1
                    pltpu.make_async_remote_copy(
                        tot.at[g, h, e], rx2.at[g, h, e], g2_s.at[g, h, e], g2_r.at[g, h, e],
                        device_id=dev(partner), device_id_type=MESH).wait_recv()
                if h == 0:
                    arrived()
                else:
                    pl.when(i >= d)(arrived)
            scale = fac_ref[0:1, 0:1] * KEEP_SCALE
            val = (own[g, h] + rx2[g, h, 0].astype(jnp.float32) + rx2[g, h, 1].astype(jnp.float32)) * scale
            cols = pl.ds(pl.multiple_of(g * 128, 128), 128)
            dkv_ref[0, h, :, cols] = val[0]
            dkv_ref[1, h, :, cols] = val[1]
        return carry

    lax.fori_loop(0, GROUPS, final, 0)
    def drain(g, carry):
        for h in range(2):
            for e in range(2):
                d = 2 * e + 2
                partner_copy(g, h, e).wait_send()
                grad1_copy(g, h, e).wait_send()
                if h == 0:
                    up_copy(g, h, d).wait_send()
                    pl.when(i >= d)(lambda d=d: grad2_copy(g, 0, d).wait_send())
                else:
                    pl.when(i >= d)(lambda d=d: up_copy(g, 1, d).wait_send())
                    grad2_copy(g, h, d).wait_send()
        return carry

    lax.fori_loop(0, GROUPS, drain, 0)


def store_kernel(o_ref, dq_ref, dkv_ref, o_hbm, dq_hbm, dk_hbm, dv_hbm, sems):
    copies = [
        pltpu.make_async_copy(o_ref, o_hbm, sems.at[0]),
        pltpu.make_async_copy(dq_ref, dq_hbm, sems.at[1]),
        pltpu.make_async_copy(dkv_ref.at[0], dk_hbm, sems.at[2]),
        pltpu.make_async_copy(dkv_ref.at[1], dv_hbm, sems.at[3]),
    ]
    for cp in copies:
        cp.start()
    for cp in copies:
        cp.wait()


def grid_of(n):
    nc, nx = 2, 4
    ny = 2 if n // (nc * nx) > 1 else 1
    return (n // (nc * nx * ny), ny, nx, nc)


def body(queries, keys, values, cotangent, doc_start, loss_mask, seeds):
    n = lax.axis_size("ctx")
    dims = grid_of(n)
    peers = max(1, dims[2] - 1, dims[1] * lax.axis_size("dp") - 1, dims[0] - 1)
    wide = (2, SPAN, HEADS * HEAD)
    narrow = (2, SPAN, GROUPS * HEAD)
    bf16, f32, i32 = jnp.bfloat16, jnp.float32, jnp.int32
    hbm = pl.BlockSpec(memory_space=pl.ANY)
    vmem = pl.BlockSpec(memory_space=pltpu.VMEM)
    dma = pltpu.SemaphoreType.DMA
    pair = (2, SPAN, HEAD)
    held = pl.pallas_call(
        functools.partial(kernel, n, dims),
        out_shape=[pltpu.VMEM(wide, bf16), pltpu.VMEM(wide, bf16), pltpu.VMEM((2,) + narrow, f32)],
        in_specs=[hbm] * 4 + [vmem, vmem, pl.BlockSpec(memory_space=pltpu.SMEM)],
        out_specs=[vmem] * 3,
        scratch_shapes=[
            pltpu.VMEM(wide, bf16),
            pltpu.VMEM(wide, bf16),
            pltpu.VMEM(wide, f32),
            pltpu.VMEM((GROUPS, 2, 5) + pair, bf16),
            pltpu.VMEM((GROUPS, 2, 5) + pair, bf16),
            pltpu.VMEM((GROUPS, 2) + pair, f32),
            pltpu.VMEM((GROUPS, 2, 2) + pair, bf16),
            pltpu.VMEM((GROUPS, 2, 2) + pair, bf16),
            pltpu.VMEM((GROUPS, 2, 2) + pair, bf16),
            pltpu.VMEM((2, HEADS // 2, 256, 128), f32),
            pltpu.VMEM((2, 256, 128), f32),
            pltpu.VMEM((2, 128, 128), bf16),
            pltpu.VMEM((320, 512), bf16),
            pltpu.VMEM((320, 512), bf16),
            pltpu.VMEM((5, 8, 128), i32),
            pltpu.VMEM((4, peers, 8, 128), i32),
            pltpu.VMEM((8, 128), f32),
            dma((2,)),
            dma((GROUPS, 2, 2)),
        ] + [dma((GROUPS, 2, 2))] * 8 + [dma((4, peers))] * 2,
        compiler_params=pltpu.CompilerParams(collective_id=0, has_side_effects=True),
        name="attention",
    )(
        queries.reshape(wide),
        cotangent.reshape(wide),
        keys.reshape(narrow),
        values.reshape(narrow),
        doc_start.reshape(2, SPAN),
        loss_mask.reshape(2, SPAN),
        seeds,
    )
    outs = pl.pallas_call(
        store_kernel,
        out_shape=[
            jax.ShapeDtypeStruct(wide, bf16),
            jax.ShapeDtypeStruct(wide, bf16),
            jax.ShapeDtypeStruct(narrow, f32),
            jax.ShapeDtypeStruct(narrow, f32),
        ],
        in_specs=[vmem] * 3,
        out_specs=[hbm] * 4,
        scratch_shapes=[dma((4,))],
        name="store",
    )(*[pltpu.with_memory_space_constraint(x, pltpu.VMEM) for x in held])
    return (
        outs[0].reshape(queries.shape),
        outs[1].reshape(queries.shape),
        outs[2].reshape(keys.shape),
        outs[3].reshape(values.shape),
    )


def solution(mesh):
    wide = P("dp", None, "ctx", None, None)
    flat = P("dp", None, "ctx", None)
    return jax.shard_map(
        body,
        mesh=mesh,
        in_specs=(wide, wide, wide, wide, flat, flat, P("dp")),
        out_specs=(wide, wide, wide, wide),
        check_vma=False,
    )
```

```python
import functools
import math

import jax
import jax.numpy as jnp
from jax import lax
from jax.experimental import pallas as pl
from jax.experimental.pallas import tpu as pltpu
from jax.sharding import PartitionSpec as P

SPAN = 64
GROUPS = 4
HEADS = 32
HEAD = 128
INV = 1.0 / math.sqrt(HEAD)
KEEP_SCALE = 1024.0 / 922.0
EXP2_SCALE = INV * math.log2(math.e)
MASKED = -1e30
MESH = pl.DeviceIdType.MESH


def nt(a, b):
    return lax.dot_general(a, b, (((1,), (1,)), ((), ())), preferred_element_type=jnp.float32)


def nn(a, b):
    return lax.dot_general(a, b, (((1,), (0,)), ((), ())), preferred_element_type=jnp.float32)


def keep_mask(mixed):
    mixed = mixed ^ lax.shift_right_arithmetic(mixed, 15)
    mixed = mixed * 73244475
    mixed = mixed ^ lax.shift_right_arithmetic(mixed, 13)
    mixed = mixed * 1274126177
    mixed = mixed ^ lax.shift_right_arithmetic(mixed, 16)
    return (mixed & 1023) >= 102


def relative_positions():
    row = lax.broadcasted_iota(jnp.int32, (256, 128), 0)
    offset = lax.broadcasted_iota(jnp.int32, (256, 128), 1) & 63
    tile = row >> 6
    inner = row & 63
    apart = jnp.where(tile == 0, 2, jnp.where(tile == 1, 1, 3))
    behind = jnp.where(tile == 3, jnp.where(inner <= offset, 0, 4), apart)
    return inner - 64 * behind


def kernel(n, dims, q_hbm, do_hbm, k_hbm, v_hbm, start_ref, mask_ref, seed_ref,
           o_ref, dqo_ref, dkv_ref,
           q_ref, do_ref,
           win, part, own, rx1, tot, rx2, keep_ref, bias_ref, mt_ref,
           s0_ref, s1_ref, d0_ref, d1_ref, pm00_ref, pm01_ref, pm10_ref, pm11_ref, ds00_ref, ds01_ref, ds10_ref, ds11_ref, sum_ref,
           acc, cbuf,
           in_sem, kv_sem,
           up_s, up_r, fw_s, fw_r, pt_s, pt_r, g1_s, g1_r, g2_s, g2_r, c_s, c_r):
    i = lax.axis_index("ctx")
    dp = lax.axis_index("dp")
    n_dp = lax.axis_size("dp")
    nz, ny, nx, nc = dims
    core = lax.rem(i, nc)
    x = lax.rem(lax.div(i, nc), nx)
    ylo = lax.rem(lax.div(i, nc * nx), ny)
    z = lax.div(i, nc * nx * ny)
    partner = i + 1 - 2 * core
    spans = (i, 2 * n - 1 - i)
    rs = (core, 1 - core)
    inside = i + 2 < n
    across = jnp.where(inside, i + 2, 2 * n - 3 - i)
    has_back = i >= 2
    inside4 = i + 4 < n
    across4 = jnp.where(inside4, i + 4, 2 * n - 5 - i)
    has_back4 = i >= 4

    def dev(c, d=dp):
        return {"ctx": c, "dp": d}

    def cidx(z_, y_, x_):
        return ((z_ * ny + y_) * nx + x_) * nc + core

    def count_peers(stage):
        peers = []
        if stage == 0:
            peers.append(dev(partner))
        elif stage == 1:
            for t in range(1, nx):
                peers.append(dev(cidx(z, ylo, lax.rem(x + t, nx))))
        elif stage == 2:
            both = dp * ny + ylo
            for t in range(1, ny * n_dp):
                other = lax.rem(both + t, ny * n_dp)
                peers.append(dev(cidx(z, lax.rem(other, ny), x), lax.div(other, ny)))
        elif stage == 3:
            for t in ((1, nz - 1, nz - 2) if nz > 4 else range(1, nz)):
                peers.append(dev(cidx(lax.rem(z + t, nz), ylo, x)))
        elif nz > 4:
            peers.append(dev(cidx(lax.rem(z + 4, nz), ylo, x)))
        return peers

    def remote(src, dst, send_sem, recv_sem, target):
        return pltpu.make_async_remote_copy(src, dst, send_sem, recv_sem, device_id=target, device_id_type=MESH)

    def count_copy(stage, t, target):
        return remote(acc.at[stage], cbuf.at[stage, t], c_s.at[stage, t], c_r.at[stage, t], target)

    def count_send(stage):
        for t, target in enumerate(count_peers(stage)):
            count_copy(stage, t, target).start()

    def count_take(stage):
        total = acc[stage]
        for t, target in enumerate(count_peers(stage)):
            cp = count_copy(stage, t, target)
            cp.wait_recv()
            cp.wait_send()
            total = total + cbuf[stage, t]
        acc[stage + 1] = total

    barrier = pltpu.get_barrier_semaphore()

    def greet(target):
        pl.semaphore_signal(barrier, inc=1, device_id=target, device_id_type=MESH)

    greet(dev(across))
    pl.when(has_back)(lambda: greet(dev(i - 2)))
    n_greet = 1
    for stage in range(4):
        for target in count_peers(stage):
            greet(target)
            n_greet += 1
    if nz > 4:
        greet(dev(cidx(lax.rem(z + 2, nz), ylo, x)))
        n_greet += 1

    ins = []
    for g in range(GROUPS):
        for h in range(2):
            for w, src in enumerate((k_hbm, v_hbm)):
                cp = pltpu.make_async_copy(src.at[h, :, pl.ds(g * 128, 128)], win.at[g, h, 0, w], kv_sem.at[g, h, w])
                cp.start()
                ins.append(cp)
    cq = pltpu.make_async_copy(q_hbm, q_ref, in_sem.at[0])
    cd = pltpu.make_async_copy(do_hbm, do_ref, in_sem.at[1])
    cq.start()
    cd.start()

    mask = mask_ref[...]
    acc[0] = jnp.pad(mask[0:1] + mask[1:2], ((0, 7), (0, 64)))

    @pl.when(i < 2)
    def _():
        zeros = jnp.zeros((GROUPS, 2, SPAN, HEAD), jnp.bfloat16)
        win[:, 0, 1] = zeros
        win[:, 0, 2] = zeros
        rx2[:, 1, 0] = zeros

    @pl.when(i < 4)
    def _():
        rx2[:, 1, 1] = jnp.zeros((GROUPS, 2, SPAN, HEAD), jnp.bfloat16)

    pl.semaphore_wait(barrier, n_greet + has_back.astype(jnp.int32))

    def up_copy(g, h, forward):
        if h == 0:
            half, target = jnp.where(inside, 0, 1), dev(across)
        else:
            half, target = 1, dev(i - 2)
        sems = (fw_s, fw_r) if forward else (up_s, up_r)
        slot = 1 if forward else 0
        return remote(win.at[g, h, slot], win.at[g, half, slot + 1], sems[0].at[g, h], sems[1].at[g, half], target)

    def up_send(g, forward):
        up_copy(g, 0, forward).start()
        pl.when(has_back)(lambda: up_copy(g, 1, forward).start())

    def up_arrived(g, h, forward):
        sems = (fw_s, fw_r) if forward else (up_s, up_r)
        slot = 2 if forward else 1
        remote(win.at[g, h, slot], win.at[g, h, slot], sems[0].at[g, h], sems[1].at[g, h], dev(partner)).wait_recv()

    def partner_copy(g, h):
        return remote(win.at[g, h, pl.ds(rs[h], 2)], win.at[g, h, pl.ds(3, 2)], pt_s.at[g, h], pt_r.at[g, h], dev(partner))

    def relay(g, forward):
        pl.when(has_back)(lambda: up_arrived(g, 0, forward))
        up_arrived(g, 1, forward)
        if not forward:
            up_send(g, True)
        else:
            for h in range(2):
                partner_copy(g, h).start()

    for g in range(GROUPS):
        for cp in ins[4 * g:4 * g + 4]:
            cp.wait()
        up_send(g, False)
    count_send(0)
    cq.wait()
    cd.wait()

    lane = lax.broadcasted_iota(jnp.int32, (1, 128), 1)
    tri = lax.broadcasted_iota(jnp.int32, (64, 128), 0) <= (lane & 63)

    def prepare(h):
        m = mask[h:h + 1].astype(jnp.float32)
        m2 = jnp.concatenate([m, m], axis=1)
        mt_ref[h] = jnp.broadcast_to(m2, (128, 128)).T.astype(jnp.bfloat16)
        rel = relative_positions()
        start_row = start_ref[h:h + 1]
        start2 = jnp.concatenate([start_row, start_row], axis=1) - spans[h] * SPAN
        bias_ref[h] = jnp.where(rel >= start2, 0.0, MASKED)
        base = seed_ref[0] * 1000003 + spans[h] * (SPAN * 9973)
        col0 = (spans[h] * SPAN + (lane & 63)) * 40503 + base + (lane >> 6) * 7919

        def fill(pair, carry):
            keep = keep_mask(relative_positions() * 9973 + (col0 + pair * (2 * 7919)))
            keep_ref[h, pair] = jnp.where(keep, 1.0, 0.0)
            for k in range(2):
                cols = pl.ds(pl.multiple_of(pair * 256 + k * 128, 128), 128)
                do_ref[h, :, cols] = do_ref[h, :, cols] * mt_ref[h, 0:64]
            return carry

        lax.fori_loop(0, HEADS // 2, fill, 0)

    prepare(0)
    count_take(0)
    count_send(1)
    relay(0, False)
    prepare(1)
    for g in range(1, GROUPS):
        relay(g, False)
    relay(0, True)
    count_take(1)
    count_send(2)

    s_refs, d_refs = (s0_ref, s1_ref), (d0_ref, d1_ref)
    pm_refs = ((pm00_ref, pm01_ref), (pm10_ref, pm11_ref))
    ds_refs = ((ds00_ref, ds01_ref), (ds10_ref, ds11_ref))

    def kv_here(g, h):
        partner_copy(g, h).wait_recv()

    def stack(ref, g, h, hh):
        return jnp.concatenate(
            [ref[h, :, pl.ds(pl.multiple_of(g * 1024 + (hh * 4 + j) * 128, 128), 128)] for j in range(4)], axis=0)

    def scores(g, h, hh, which=(0, 1)):
        if 0 in which:
            s_refs[hh][...] = nt(win[g, h, :, 0].reshape(320, 128), stack(q_ref, g, h, hh))
        if 1 in which:
            d_refs[hh][...] = nt(win[g, h, :, 1].reshape(320, 128), stack(do_ref, g, h, hh))

    def soft(g, h, hh, prs=(0, 1)):
        s_ref, d_ref = s_refs[hh], d_refs[hh]
        for pr in prs:
            cs = slice(pr * 128, pr * 128 + 128)
            s = jnp.concatenate([s_ref[64:128, cs], s_ref[192:320, cs], jnp.where(tri, s_ref[0:64, cs], s_ref[128:192, cs])], axis=0)
            s = s + bias_ref[h]
            top = jnp.max(s, axis=0, keepdims=True)
            e = jnp.exp2((s - top) * EXP2_SCALE)
            p = e * (1.0 / jnp.sum(e, axis=0, keepdims=True))
            pm = p * keep_ref[h, g * 4 + hh * 2 + pr]
            dpv = jnp.concatenate([d_ref[64:128, cs], d_ref[192:320, cs], jnp.where(tri, d_ref[0:64, cs], d_ref[128:192, cs])], axis=0)
            t = pm * dpv
            ds = t - p * jnp.sum(t, axis=0, keepdims=True)
            for ref, val in ((pm_refs[h][hh], pm), (ds_refs[h][hh], ds)):
                ref[g, 0:64, cs] = jnp.where(tri, val[192:], 0.0).astype(jnp.bfloat16)
                ref[g, 64:128, cs] = val[:64].astype(jnp.bfloat16)
                ref[g, 128:192, cs] = jnp.where(tri, 0.0, val[192:]).astype(jnp.bfloat16)
                ref[g, 192:320, cs] = val[64:192].astype(jnp.bfloat16)

    def products(g, h, hh):
        for w, (ref, other) in enumerate(((ds_refs[h][hh], q_ref), (pm_refs[h][hh], do_ref))):
            val = nn(ref[g], stack(other, g, h, hh))
            if hh == 0:
                sum_ref[w] = val
            else:
                val = val + sum_ref[w]
                own[g, h, w] = val[0:64]
                part[g, h, :, w] = val.reshape(5, SPAN, HEAD).astype(jnp.bfloat16)

    def outputs(g, h):
        kt = win[g, h, :, 0].reshape(320, 128).T
        vt = win[g, h, :, 1].reshape(320, 128).T
        for hh in range(2):
            oo = (nn(vt, pm_refs[h][hh][g]) * KEEP_SCALE).astype(jnp.bfloat16).T
            dq = nn(kt, ds_refs[h][hh][g]).astype(jnp.bfloat16).T
            for j in range(4):
                cols = pl.ds(pl.multiple_of(g * 1024 + (hh * 4 + j) * 128, 128), 128)
                o_ref[h, :, cols] = oo[j * 64:(j + 1) * 64]
                dqo_ref[h, :, cols] = dq[j * 64:(j + 1) * 64]

    def block(sc, so, pr):
        products(*pr)
        soft(*so)
        scores(*sc)

    def grad1_copy(g, h):
        return remote(part.at[g, h, pl.ds(3, 2)], rx1.at[g, h], g1_s.at[g, h], g1_r.at[g, h], dev(partner))

    def share(g, h):
        grad1_copy(g, h).start()

    def down_copy(g, h, e):
        if h == 0:
            half, target = 0, dev(i - 2 - 2 * e)
        else:
            half = jnp.where((inside, inside4)[e], 1, 0)
            target = dev((across, across4)[e])
        return remote(tot.at[g, h, e], rx2.at[g, half, e], g2_s.at[g, h, e], g2_r.at[g, half, e], target)

    def down_arrived(g, h, e):
        def take():
            remote(rx2.at[g, h, e], rx2.at[g, h, e], g2_s.at[g, h, e], g2_r.at[g, h, e], dev(partner)).wait_recv()

        if h == 0:
            take()
        else:
            pl.when((has_back, has_back4)[e])(take)

    def combine(g, h):
        r = rs[h]
        grad1_copy(g, h).wait_recv()
        tot[g, h, 1] = part[g, h, 2] + rx1[g, h, 1] * r.astype(jnp.bfloat16)
        tot[g, h, 0] = part[g, h, 1] + rx1[g, h, 1 - r]
        for e in (1, 0):
            if h == 0:
                pl.when((has_back, has_back4)[e])(lambda e=e: down_copy(g, h, e).start())
            else:
                down_copy(g, h, e).start()

    kv_here(0, 0)
    scores(0, 0, 0)
    pm11_ref[0] = jnp.zeros((320, 256), jnp.bfloat16)
    ds11_ref[0] = jnp.zeros((320, 256), jnp.bfloat16)

    def step(g, carry):
        before = jnp.maximum(g - 1, 0)
        after = jnp.minimum(g + 1, GROUPS - 1)
        block((g, 0, 1), (g, 0, 0), (before, 1, 1))

        @pl.when(g > 0)
        def _():
            share(g - 1, 1)
            combine(g - 1, 0)

        pl.when(g < GROUPS - 1)(lambda: relay(g + 1, True))
        kv_here(g, 1)
        block((g, 1, 0), (g, 0, 1), (g, 0, 0))
        block((g, 1, 1), (g, 1, 0), (g, 0, 1))
        share(g, 0)
        pl.when(g > 0)(lambda: combine(g - 1, 1))

        @pl.when(g == 1)
        def _():
            count_take(2)
            count_send(3)

        @pl.when(g == 3)
        def _():
            count_take(3)
            count_send(4)

        pl.when(g < GROUPS - 1)(lambda: kv_here(g + 1, 0))
        block((after, 0, 0), (g, 1, 1), (g, 1, 0))
        return carry

    lax.fori_loop(0, GROUPS, step, 0)
    products(GROUPS - 1, 1, 1)
    share(GROUPS - 1, 1)
    combine(GROUPS - 1, 0)
    def finish(g, carry):
        for h in range(2):
            outputs(g, h)
        return carry

    finish(0, 0)
    combine(GROUPS - 1, 1)
    lax.fori_loop(1, GROUPS, finish, 0)

    def drain(g, carry):
        for h in range(2):
            partner_copy(g, h).wait_send()
            grad1_copy(g, h).wait_send()
            down_copy(g, 1, h).wait_send()
            pl.when((has_back, has_back4)[h])(lambda h=h: down_copy(g, 0, h).wait_send())
        for flag in (False, True):
            up_copy(g, 0, flag).wait_send()
            pl.when(has_back)(lambda flag=flag: up_copy(g, 1, flag).wait_send())
        return carry

    lax.fori_loop(0, GROUPS, drain, 0)

    for g in range(GROUPS):
        for h in range(2):
            for e in range(2):
                down_arrived(g, h, e)
    count_take(4)
    total = jnp.sum(acc[5].astype(jnp.float32))
    slots = float(2 * 2 * n * SPAN)
    factor = jnp.full((1, 128), slots * KEEP_SCALE, jnp.float32) / jnp.full((1, 128), total, jnp.float32)

    def final(g, carry):
        for h in range(2):
            val = own[g, h] + (1 - rs[h]).astype(jnp.float32) * rx1[g, h, 0].astype(jnp.float32)
            val = val + rx2[g, h, 0].astype(jnp.float32) + rx2[g, h, 1].astype(jnp.float32)
            cols = pl.ds(pl.multiple_of(g * 128, 128), 128)
            dkv_ref[0, h, :, cols] = val[0] * (factor * INV)
            dkv_ref[1, h, :, cols] = val[1] * factor
            for j in range(8):
                cols = pl.ds(pl.multiple_of(g * 1024 + j * 128, 128), 128)
                dqo_ref[h, :, cols] = (dqo_ref[h, :, cols].astype(jnp.float32) * (factor * INV)).astype(jnp.bfloat16)
        return carry

    lax.fori_loop(0, GROUPS, final, 0)


def store_kernel(o_ref, dq_ref, dkv_ref, o_hbm, dq_hbm, dk_hbm, dv_hbm, sems):
    copies = [
        pltpu.make_async_copy(o_ref, o_hbm, sems.at[0]),
        pltpu.make_async_copy(dq_ref, dq_hbm, sems.at[1]),
        pltpu.make_async_copy(dkv_ref.at[0], dk_hbm, sems.at[2]),
        pltpu.make_async_copy(dkv_ref.at[1], dv_hbm, sems.at[3]),
    ]
    for cp in copies:
        cp.start()
    for cp in copies:
        cp.wait()


def grid_of(n):
    nc, nx = 2, 4
    ny = 2 if n // (nc * nx) > 1 else 1
    return (n // (nc * nx * ny), ny, nx, nc)


def body(queries, keys, values, cotangent, doc_start, loss_mask, seeds):
    n = lax.axis_size("ctx")
    dims = grid_of(n)
    peers = max(1, dims[2] - 1, dims[1] * lax.axis_size("dp") - 1, dims[0] - 1)
    wide = (2, SPAN, HEADS * HEAD)
    narrow = (2, SPAN, GROUPS * HEAD)
    bf16, f32, i32 = jnp.bfloat16, jnp.float32, jnp.int32
    hbm = pl.BlockSpec(memory_space=pl.ANY)
    vmem = pl.BlockSpec(memory_space=pltpu.VMEM)
    dma = pltpu.SemaphoreType.DMA
    pair = (2, SPAN, HEAD)
    held = pl.pallas_call(
        functools.partial(kernel, n, dims),
        out_shape=[pltpu.VMEM(wide, bf16), pltpu.VMEM(wide, bf16), pltpu.VMEM((2,) + narrow, f32)],
        in_specs=[hbm] * 4 + [vmem, vmem, pl.BlockSpec(memory_space=pltpu.SMEM)],
        out_specs=[vmem] * 3,
        scratch_shapes=[
            pltpu.VMEM(wide, bf16),
            pltpu.VMEM(wide, bf16),
            pltpu.VMEM((GROUPS, 2, 5) + pair, bf16),
            pltpu.VMEM((GROUPS, 2, 5) + pair, bf16),
            pltpu.VMEM((GROUPS, 2) + pair, f32),
            pltpu.VMEM((GROUPS, 2, 2) + pair, bf16),
            pltpu.VMEM((GROUPS, 2, 2) + pair, bf16),
            pltpu.VMEM((GROUPS, 2, 2) + pair, bf16),
            pltpu.VMEM((2, HEADS // 2, 256, 128), f32),
            pltpu.VMEM((2, 256, 128), f32),
            pltpu.VMEM((2, 128, 128), bf16),
        ] + [pltpu.VMEM((320, 256), f32)] * 4 + [pltpu.VMEM((GROUPS, 320, 256), bf16)] * 8 + [
            pltpu.VMEM((2, 320, 128), f32),
            pltpu.VMEM((6, 8, 128), i32),
            pltpu.VMEM((5, peers, 8, 128), i32),
            dma((2,)),
            dma((GROUPS, 2, 2)),
        ] + [dma((GROUPS, 2))] * 8 + [dma((GROUPS, 2, 2))] * 2 + [dma((5, peers))] * 2,
        compiler_params=pltpu.CompilerParams(collective_id=0, has_side_effects=True),
        name="attention",
    )(
        queries.reshape(wide),
        cotangent.reshape(wide),
        keys.reshape(narrow),
        values.reshape(narrow),
        doc_start.reshape(2, SPAN),
        loss_mask.reshape(2, SPAN),
        seeds,
    )
    outs = pl.pallas_call(
        store_kernel,
        out_shape=[
            jax.ShapeDtypeStruct(wide, bf16),
            jax.ShapeDtypeStruct(wide, bf16),
            jax.ShapeDtypeStruct(narrow, f32),
            jax.ShapeDtypeStruct(narrow, f32),
        ],
        in_specs=[vmem] * 3,
        out_specs=[hbm] * 4,
        scratch_shapes=[dma((4,))],
        name="store",
    )(*[pltpu.with_memory_space_constraint(x, pltpu.VMEM) for x in held])
    return (
        outs[0].reshape(queries.shape),
        outs[1].reshape(queries.shape),
        outs[2].reshape(keys.shape),
        outs[3].reshape(values.shape),
    )


def solution(mesh):
    wide = P("dp", None, "ctx", None, None)
    flat = P("dp", None, "ctx", None)
    return jax.shard_map(
        body,
        mesh=mesh,
        in_specs=(wide, wide, wide, wide, flat, flat, P("dp")),
        out_specs=(wide, wide, wide, wide),
        check_vma=False,
    )
```

```python
import functools
import math

import jax
import jax.numpy as jnp
from jax import lax
from jax.experimental import pallas as pl
from jax.experimental.pallas import tpu as pltpu
from jax.sharding import PartitionSpec as P

SPAN = 64
GROUPS = 4
HEADS = 32
HEAD = 128
INV = 1.0 / math.sqrt(HEAD)
KEEP_SCALE = 1024.0 / 922.0
EXP2_SCALE = INV * math.log2(math.e)
MASKED = -1e30
MESH = pl.DeviceIdType.MESH


def nt(a, b):
    return lax.dot_general(a, b, (((1,), (1,)), ((), ())), preferred_element_type=jnp.float32)


def nn(a, b):
    return lax.dot_general(a, b, (((1,), (0,)), ((), ())), preferred_element_type=jnp.float32)


def keep_mask(mixed):
    mixed = mixed ^ lax.shift_right_arithmetic(mixed, 15)
    mixed = mixed * 73244475
    mixed = mixed ^ lax.shift_right_arithmetic(mixed, 13)
    mixed = mixed * 1274126177
    mixed = mixed ^ lax.shift_right_arithmetic(mixed, 16)
    return (mixed & 1023) >= 102


def relative_positions():
    row = lax.broadcasted_iota(jnp.int32, (256, 128), 0)
    offset = lax.broadcasted_iota(jnp.int32, (256, 128), 1) & 63
    tile = row >> 6
    inner = row & 63
    apart = jnp.where(tile == 0, 2, jnp.where(tile == 1, 1, 3))
    behind = jnp.where(tile == 3, jnp.where(inner <= offset, 0, 4), apart)
    return inner - 64 * behind


def kernel(n, dims, q_hbm, do_hbm, k_hbm, v_hbm, start_hbm, mask_hbm, seed_hbm,
           o_ref, dqo_ref, dkv_ref,
           q_ref, do_ref, start_ref, mask_ref, seed_ref,
           win, part, own, rx1, tot, rx2, keep_ref, bias_ref, mt_ref,
           s0_ref, s1_ref, d0_ref, d1_ref, pm00_ref, pm01_ref, pm10_ref, pm11_ref, ds00_ref, ds01_ref, ds10_ref, ds11_ref, sum_ref,
           acc, cbuf,
           in_sem, kv_sem,
           up_s, up_r, fw_s, fw_r, pt_s, pt_r, g1_s, g1_r, g2_s, g2_r, c_s, c_r):
    i = lax.axis_index("ctx")
    dp = lax.axis_index("dp")
    n_dp = lax.axis_size("dp")
    nz, ny, nx, nc = dims
    core = lax.rem(i, nc)
    x = lax.rem(lax.div(i, nc), nx)
    ylo = lax.rem(lax.div(i, nc * nx), ny)
    z = lax.div(i, nc * nx * ny)
    partner = i + 1 - 2 * core
    spans = (i, 2 * n - 1 - i)
    rs = (core, 1 - core)
    inside = i + 2 < n
    across = jnp.where(inside, i + 2, 2 * n - 3 - i)
    has_back = i >= 2
    inside4 = i + 4 < n
    across4 = jnp.where(inside4, i + 4, 2 * n - 5 - i)
    has_back4 = i >= 4

    def dev(c, d=dp):
        return {"ctx": c, "dp": d}

    def cidx(z_, y_, x_):
        return ((z_ * ny + y_) * nx + x_) * nc + core

    def count_peers(stage):
        peers = []
        if stage == 0:
            peers.append(dev(partner))
        elif stage == 1:
            for t in range(1, nx):
                peers.append(dev(cidx(z, ylo, lax.rem(x + t, nx))))
        elif stage == 2:
            both = dp * ny + ylo
            for t in range(1, ny * n_dp):
                other = lax.rem(both + t, ny * n_dp)
                peers.append(dev(cidx(z, lax.rem(other, ny), x), lax.div(other, ny)))
        elif stage == 3:
            for t in ((1, nz - 1, nz - 2) if nz > 4 else range(1, nz)):
                peers.append(dev(cidx(lax.rem(z + t, nz), ylo, x)))
        elif nz > 4:
            peers.append(dev(cidx(lax.rem(z + 4, nz), ylo, x)))
        return peers

    def remote(src, dst, send_sem, recv_sem, target):
        return pltpu.make_async_remote_copy(src, dst, send_sem, recv_sem, device_id=target, device_id_type=MESH)

    def count_copy(stage, t, target):
        return remote(acc.at[stage], cbuf.at[stage, t], c_s.at[stage, t], c_r.at[stage, t], target)

    def count_send(stage):
        for t, target in enumerate(count_peers(stage)):
            count_copy(stage, t, target).start()

    def count_take(stage):
        total = acc[stage]
        for t, target in enumerate(count_peers(stage)):
            cp = count_copy(stage, t, target)
            cp.wait_recv()
            cp.wait_send()
            total = total + cbuf[stage, t]
        acc[stage + 1] = total

    barrier = pltpu.get_barrier_semaphore()

    def greet(target):
        pl.semaphore_signal(barrier, inc=1, device_id=target, device_id_type=MESH)

    greet(dev(across))
    pl.when(has_back)(lambda: greet(dev(i - 2)))
    n_greet = 1
    for stage in range(4):
        for target in count_peers(stage):
            greet(target)
            n_greet += 1
    if nz > 4:
        greet(dev(cidx(lax.rem(z + 2, nz), ylo, x)))
        n_greet += 1

    ins = []
    for g in range(GROUPS):
        for h in range(2):
            for w, src in enumerate((k_hbm, v_hbm)):
                cp = pltpu.make_async_copy(src.at[h, :, pl.ds(g * 128, 128)], win.at[g, h, 0, w], kv_sem.at[g, h, w])
                cp.start()
                ins.append(cp)
    cq = pltpu.make_async_copy(q_hbm, q_ref, in_sem.at[0])
    cd = pltpu.make_async_copy(do_hbm, do_ref, in_sem.at[1])
    small = [
        pltpu.make_async_copy(src, dst, in_sem.at[2 + k])
        for k, (src, dst) in enumerate(((start_hbm, start_ref), (mask_hbm, mask_ref), (seed_hbm, seed_ref)))
    ]
    for cp in small:
        cp.start()
    cq.start()
    cd.start()


    @pl.when(i < 2)
    def _():
        zeros = jnp.zeros((GROUPS, 2, SPAN, HEAD), jnp.bfloat16)
        win[:, 0, 1] = zeros
        win[:, 0, 2] = zeros
        rx2[:, 1, 0] = zeros

    @pl.when(i < 4)
    def _():
        rx2[:, 1, 1] = jnp.zeros((GROUPS, 2, SPAN, HEAD), jnp.bfloat16)

    pl.semaphore_wait(barrier, n_greet + has_back.astype(jnp.int32))

    def up_copy(g, h, forward):
        if h == 0:
            half, target = jnp.where(inside, 0, 1), dev(across)
        else:
            half, target = 1, dev(i - 2)
        sems = (fw_s, fw_r) if forward else (up_s, up_r)
        slot = 1 if forward else 0
        return remote(win.at[g, h, slot], win.at[g, half, slot + 1], sems[0].at[g, h], sems[1].at[g, half], target)

    def up_send(g, forward):
        up_copy(g, 0, forward).start()
        pl.when(has_back)(lambda: up_copy(g, 1, forward).start())

    def up_arrived(g, h, forward):
        sems = (fw_s, fw_r) if forward else (up_s, up_r)
        slot = 2 if forward else 1
        remote(win.at[g, h, slot], win.at[g, h, slot], sems[0].at[g, h], sems[1].at[g, h], dev(partner)).wait_recv()

    def partner_copy(g, h):
        return remote(win.at[g, h, pl.ds(rs[h], 2)], win.at[g, h, pl.ds(3, 2)], pt_s.at[g, h], pt_r.at[g, h], dev(partner))

    def relay(g, forward):
        pl.when(has_back)(lambda: up_arrived(g, 0, forward))
        up_arrived(g, 1, forward)
        if not forward:
            up_send(g, True)
        else:
            for h in range(2):
                partner_copy(g, h).start()

    for g in range(GROUPS):
        for cp in ins[4 * g:4 * g + 4]:
            cp.wait()
        up_send(g, False)
    for cp in small:
        cp.wait()
    mask = mask_ref[...]
    acc[0] = jnp.pad(mask[0:1] + mask[1:2], ((0, 7), (0, 64)))
    count_send(0)
    cq.wait()
    cd.wait()

    lane = lax.broadcasted_iota(jnp.int32, (1, 128), 1)
    tri = lax.broadcasted_iota(jnp.int32, (64, 128), 0) <= (lane & 63)

    def prepare(h):
        m = mask[h:h + 1].astype(jnp.float32)
        m2 = jnp.concatenate([m, m], axis=1)
        mt_ref[h] = jnp.broadcast_to(m2, (128, 128)).T.astype(jnp.bfloat16)
        rel = relative_positions()
        start_row = start_ref[h:h + 1]
        start2 = jnp.concatenate([start_row, start_row], axis=1) - spans[h] * SPAN
        bias_ref[h] = jnp.where(rel >= start2, 0.0, MASKED)
        base = seed_ref[0] * 1000003 + spans[h] * (SPAN * 9973)
        col0 = (spans[h] * SPAN + (lane & 63)) * 40503 + base + (lane >> 6) * 7919

        def fill(pair, carry):
            keep = keep_mask(relative_positions() * 9973 + (col0 + pair * (2 * 7919)))
            keep_ref[h, pair] = jnp.where(keep, 1.0, 0.0)
            for k in range(2):
                cols = pl.ds(pl.multiple_of(pair * 256 + k * 128, 128), 128)
                do_ref[h, :, cols] = do_ref[h, :, cols] * mt_ref[h, 0:64]
            return carry

        lax.fori_loop(0, HEADS // 2, fill, 0)

    prepare(0)
    count_take(0)
    count_send(1)
    relay(0, False)
    prepare(1)
    for g in range(1, GROUPS):
        relay(g, False)
    relay(0, True)
    count_take(1)
    count_send(2)

    s_refs, d_refs = (s0_ref, s1_ref), (d0_ref, d1_ref)
    pm_refs = ((pm00_ref, pm01_ref), (pm10_ref, pm11_ref))
    ds_refs = ((ds00_ref, ds01_ref), (ds10_ref, ds11_ref))

    def kv_here(g, h):
        partner_copy(g, h).wait_recv()

    def stack(ref, g, h, hh):
        return jnp.concatenate(
            [ref[h, :, pl.ds(pl.multiple_of(g * 1024 + (hh * 4 + j) * 128, 128), 128)] for j in range(4)], axis=0)

    def scores(g, h, hh, which=(0, 1)):
        if 0 in which:
            s_refs[hh][...] = nt(win[g, h, :, 0].reshape(320, 128), stack(q_ref, g, h, hh))
        if 1 in which:
            d_refs[hh][...] = nt(win[g, h, :, 1].reshape(320, 128), stack(do_ref, g, h, hh))

    def soft(g, h, hh, prs=(0, 1)):
        s_ref, d_ref = s_refs[hh], d_refs[hh]
        for pr in prs:
            cs = slice(pr * 128, pr * 128 + 128)
            s = jnp.concatenate([s_ref[64:128, cs], s_ref[192:320, cs], jnp.where(tri, s_ref[0:64, cs], s_ref[128:192, cs])], axis=0)
            s = s + bias_ref[h]
            top = jnp.max(s, axis=0, keepdims=True)
            e = jnp.exp2((s - top) * EXP2_SCALE)
            p = e * (1.0 / jnp.sum(e, axis=0, keepdims=True))
            pm = p * keep_ref[h, g * 4 + hh * 2 + pr]
            dpv = jnp.concatenate([d_ref[64:128, cs], d_ref[192:320, cs], jnp.where(tri, d_ref[0:64, cs], d_ref[128:192, cs])], axis=0)
            t = pm * dpv
            ds = t - p * jnp.sum(t, axis=0, keepdims=True)
            for ref, val in ((pm_refs[h][hh], pm), (ds_refs[h][hh], ds)):
                ref[g, 0:64, cs] = jnp.where(tri, val[192:], 0.0).astype(jnp.bfloat16)
                ref[g, 64:128, cs] = val[:64].astype(jnp.bfloat16)
                ref[g, 128:192, cs] = jnp.where(tri, 0.0, val[192:]).astype(jnp.bfloat16)
                ref[g, 192:320, cs] = val[64:192].astype(jnp.bfloat16)

    def products(g, h, hh):
        for w, (ref, other) in enumerate(((ds_refs[h][hh], q_ref), (pm_refs[h][hh], do_ref))):
            val = nn(ref[g], stack(other, g, h, hh))
            if hh == 0:
                sum_ref[w] = val
            else:
                val = val + sum_ref[w]
                own[g, h, w] = val[0:64]
                part[g, h, :, w] = val.reshape(5, SPAN, HEAD).astype(jnp.bfloat16)

    def outputs(g, h):
        kt = win[g, h, :, 0].reshape(320, 128).T
        vt = win[g, h, :, 1].reshape(320, 128).T
        for hh in range(2):
            oo = (nn(vt, pm_refs[h][hh][g]) * KEEP_SCALE).astype(jnp.bfloat16).T
            dq = nn(kt, ds_refs[h][hh][g]).astype(jnp.bfloat16).T
            for j in range(4):
                cols = pl.ds(pl.multiple_of(g * 1024 + (hh * 4 + j) * 128, 128), 128)
                o_ref[h, :, cols] = oo[j * 64:(j + 1) * 64]
                dqo_ref[h, :, cols] = dq[j * 64:(j + 1) * 64]

    def block(sc, so, pr):
        products(*pr)
        soft(*so)
        scores(*sc)

    def grad1_copy(g, h):
        return remote(part.at[g, h, pl.ds(3, 2)], rx1.at[g, h], g1_s.at[g, h], g1_r.at[g, h], dev(partner))

    def share(g, h):
        grad1_copy(g, h).start()

    def down_copy(g, h, e):
        if h == 0:
            half, target = 0, dev(i - 2 - 2 * e)
        else:
            half = jnp.where((inside, inside4)[e], 1, 0)
            target = dev((across, across4)[e])
        return remote(tot.at[g, h, e], rx2.at[g, half, e], g2_s.at[g, h, e], g2_r.at[g, half, e], target)

    def down_arrived(g, h, e):
        def take():
            remote(rx2.at[g, h, e], rx2.at[g, h, e], g2_s.at[g, h, e], g2_r.at[g, h, e], dev(partner)).wait_recv()

        if h == 0:
            take()
        else:
            pl.when((has_back, has_back4)[e])(take)

    def combine(g, h):
        r = rs[h]
        grad1_copy(g, h).wait_recv()
        tot[g, h, 1] = part[g, h, 2] + rx1[g, h, 1] * r.astype(jnp.bfloat16)
        tot[g, h, 0] = part[g, h, 1] + rx1[g, h, 1 - r]
        for e in (1, 0):
            if h == 0:
                pl.when((has_back, has_back4)[e])(lambda e=e: down_copy(g, h, e).start())
            else:
                down_copy(g, h, e).start()

    kv_here(0, 0)
    scores(0, 0, 0)
    pm11_ref[0] = jnp.zeros((320, 256), jnp.bfloat16)
    ds11_ref[0] = jnp.zeros((320, 256), jnp.bfloat16)

    def step(g, carry):
        before = jnp.maximum(g - 1, 0)
        after = jnp.minimum(g + 1, GROUPS - 1)
        block((g, 0, 1), (g, 0, 0), (before, 1, 1))

        @pl.when(g > 0)
        def _():
            share(g - 1, 1)
            combine(g - 1, 0)

        pl.when(g < GROUPS - 1)(lambda: relay(g + 1, True))
        kv_here(g, 1)
        block((g, 1, 0), (g, 0, 1), (g, 0, 0))
        block((g, 1, 1), (g, 1, 0), (g, 0, 1))
        share(g, 0)
        pl.when(g > 0)(lambda: combine(g - 1, 1))

        @pl.when(g == 1)
        def _():
            count_take(2)
            count_send(3)

        @pl.when(g == 3)
        def _():
            count_take(3)
            count_send(4)

        pl.when(g < GROUPS - 1)(lambda: kv_here(g + 1, 0))
        block((after, 0, 0), (g, 1, 1), (g, 1, 0))
        return carry

    lax.fori_loop(0, GROUPS, step, 0)
    products(GROUPS - 1, 1, 1)
    share(GROUPS - 1, 1)
    combine(GROUPS - 1, 0)
    def finish(g, carry):
        for h in range(2):
            outputs(g, h)
        return carry

    finish(0, 0)
    combine(GROUPS - 1, 1)
    lax.fori_loop(1, GROUPS, finish, 0)

    def drain(g, carry):
        for h in range(2):
            partner_copy(g, h).wait_send()
            grad1_copy(g, h).wait_send()
            down_copy(g, 1, h).wait_send()
            pl.when((has_back, has_back4)[h])(lambda h=h: down_copy(g, 0, h).wait_send())
        for flag in (False, True):
            up_copy(g, 0, flag).wait_send()
            pl.when(has_back)(lambda flag=flag: up_copy(g, 1, flag).wait_send())
        return carry

    lax.fori_loop(0, GROUPS, drain, 0)

    def arrived(g):
        for h in range(2):
            for e in range(2):
                down_arrived(g, h, e)

    for g in range(GROUPS - 1):
        arrived(g)
    count_take(4)
    total = jnp.sum(acc[5].astype(jnp.float32))
    slots = float(2 * 2 * n * SPAN)
    factor = jnp.full((1, 128), slots * KEEP_SCALE, jnp.float32) / jnp.full((1, 128), total, jnp.float32)

    def rescale(g, carry):
        for h in range(2):
            for j in range(8):
                cols = pl.ds(pl.multiple_of(g * 1024 + j * 128, 128), 128)
                dqo_ref[h, :, cols] = (dqo_ref[h, :, cols].astype(jnp.float32) * (factor * INV)).astype(jnp.bfloat16)
        return carry

    def final(g, carry):
        for h in range(2):
            val = own[g, h] + (1 - rs[h]).astype(jnp.float32) * rx1[g, h, 0].astype(jnp.float32)
            val = val + rx2[g, h, 0].astype(jnp.float32) + rx2[g, h, 1].astype(jnp.float32)
            cols = pl.ds(pl.multiple_of(g * 128, 128), 128)
            dkv_ref[0, h, :, cols] = val[0] * (factor * INV)
            dkv_ref[1, h, :, cols] = val[1] * factor
        return carry

    lax.fori_loop(0, GROUPS, rescale, 0)
    lax.fori_loop(0, GROUPS - 1, final, 0)
    arrived(GROUPS - 1)
    final(GROUPS - 1, 0)


def store_kernel(o_ref, dq_ref, dkv_ref, o_hbm, dq_hbm, dk_hbm, dv_hbm, sems):
    copies = [
        pltpu.make_async_copy(o_ref, o_hbm, sems.at[0]),
        pltpu.make_async_copy(dq_ref, dq_hbm, sems.at[1]),
        pltpu.make_async_copy(dkv_ref.at[0], dk_hbm, sems.at[2]),
        pltpu.make_async_copy(dkv_ref.at[1], dv_hbm, sems.at[3]),
    ]
    for cp in copies:
        cp.start()
    for cp in copies:
        cp.wait()


def grid_of(n):
    nc, nx = 2, 4
    ny = 2 if n // (nc * nx) > 1 else 1
    return (n // (nc * nx * ny), ny, nx, nc)


def body(queries, keys, values, cotangent, doc_start, loss_mask, seeds):
    n = lax.axis_size("ctx")
    dims = grid_of(n)
    peers = max(1, dims[2] - 1, dims[1] * lax.axis_size("dp") - 1, dims[0] - 1)
    wide = (2, SPAN, HEADS * HEAD)
    narrow = (2, SPAN, GROUPS * HEAD)
    bf16, f32, i32 = jnp.bfloat16, jnp.float32, jnp.int32
    hbm = pl.BlockSpec(memory_space=pl.ANY)
    vmem = pl.BlockSpec(memory_space=pltpu.VMEM)
    dma = pltpu.SemaphoreType.DMA
    pair = (2, SPAN, HEAD)
    held = pl.pallas_call(
        functools.partial(kernel, n, dims),
        out_shape=[pltpu.VMEM(wide, bf16), pltpu.VMEM(wide, bf16), pltpu.VMEM((2,) + narrow, f32)],
        in_specs=[hbm] * 7,
        out_specs=[vmem] * 3,
        scratch_shapes=[
            pltpu.VMEM(wide, bf16),
            pltpu.VMEM(wide, bf16),
            pltpu.VMEM((2, SPAN), i32),
            pltpu.VMEM((2, SPAN), i32),
            pltpu.SMEM((1,), i32),
            pltpu.VMEM((GROUPS, 2, 5) + pair, bf16),
            pltpu.VMEM((GROUPS, 2, 5) + pair, bf16),
            pltpu.VMEM((GROUPS, 2) + pair, f32),
            pltpu.VMEM((GROUPS, 2, 2) + pair, bf16),
            pltpu.VMEM((GROUPS, 2, 2) + pair, bf16),
            pltpu.VMEM((GROUPS, 2, 2) + pair, bf16),
            pltpu.VMEM((2, HEADS // 2, 256, 128), f32),
            pltpu.VMEM((2, 256, 128), f32),
            pltpu.VMEM((2, 128, 128), bf16),
        ] + [pltpu.VMEM((320, 256), f32)] * 4 + [pltpu.VMEM((GROUPS, 320, 256), bf16)] * 8 + [
            pltpu.VMEM((2, 320, 128), f32),
            pltpu.VMEM((6, 8, 128), i32),
            pltpu.VMEM((5, peers, 8, 128), i32),
            dma((5,)),
            dma((GROUPS, 2, 2)),
        ] + [dma((GROUPS, 2))] * 8 + [dma((GROUPS, 2, 2))] * 2 + [dma((5, peers))] * 2,
        compiler_params=pltpu.CompilerParams(collective_id=0, has_side_effects=True),
        name="attention",
    )(
        queries.reshape(wide),
        cotangent.reshape(wide),
        keys.reshape(narrow),
        values.reshape(narrow),
        doc_start.reshape(2, SPAN),
        loss_mask.reshape(2, SPAN),
        seeds,
    )
    outs = pl.pallas_call(
        store_kernel,
        out_shape=[
            jax.ShapeDtypeStruct(wide, bf16),
            jax.ShapeDtypeStruct(wide, bf16),
            jax.ShapeDtypeStruct(narrow, f32),
            jax.ShapeDtypeStruct(narrow, f32),
        ],
        in_specs=[vmem] * 3,
        out_specs=[hbm] * 4,
        scratch_shapes=[dma((4,))],
        name="store",
    )(*[pltpu.with_memory_space_constraint(x, pltpu.VMEM) for x in held])
    return (
        outs[0].reshape(queries.shape),
        outs[1].reshape(queries.shape),
        outs[2].reshape(keys.shape),
        outs[3].reshape(values.shape),
    )


def solution(mesh):
    wide = P("dp", None, "ctx", None, None)
    flat = P("dp", None, "ctx", None)
    return jax.shard_map(
        body,
        mesh=mesh,
        in_specs=(wide, wide, wide, wide, flat, flat, P("dp")),
        out_specs=(wide, wide, wide, wide),
        check_vma=False,
    )
```

```python
import functools
import math

import jax
import jax.numpy as jnp
from jax import lax
from jax.experimental import pallas as pl
from jax.experimental.pallas import tpu as pltpu
from jax.sharding import PartitionSpec as P

SPAN = 64
GROUPS = 4
HEADS = 32
HEAD = 128
INV = 1.0 / math.sqrt(HEAD)
KEEP_SCALE = 1024.0 / 922.0
EXP2_SCALE = INV * math.log2(math.e)
MASKED = -1e30
MESH = pl.DeviceIdType.MESH


def nt(a, b):
    return lax.dot_general(a, b, (((1,), (1,)), ((), ())), preferred_element_type=jnp.float32)


def nn(a, b):
    return lax.dot_general(a, b, (((1,), (0,)), ((), ())), preferred_element_type=jnp.float32)


def keep_mask(mixed):
    mixed = mixed ^ lax.shift_right_arithmetic(mixed, 15)
    mixed = mixed * 73244475
    mixed = mixed ^ lax.shift_right_arithmetic(mixed, 13)
    mixed = mixed * 1274126177
    mixed = mixed ^ lax.shift_right_arithmetic(mixed, 16)
    return (mixed & 1023) >= 102


def relative_positions():
    row = lax.broadcasted_iota(jnp.int32, (256, 128), 0)
    offset = lax.broadcasted_iota(jnp.int32, (256, 128), 1) & 63
    tile = row >> 6
    inner = row & 63
    apart = jnp.where(tile == 0, 2, jnp.where(tile == 1, 1, 3))
    behind = jnp.where(tile == 3, jnp.where(inner <= offset, 0, 4), apart)
    return inner - 64 * behind


def kernel(n, dims, q_hbm, do_hbm, k_hbm, v_hbm, start_hbm, mask_hbm, seed_hbm,
           o_ref, dqo_ref, dkv_ref,
           q_ref, do_ref, start_ref, mask_ref, seed_ref,
           win, part, own, rx1, tot, rx2, keep_ref, bias_ref, mt_ref,
           s0_ref, s1_ref, d0_ref, d1_ref, pm00_ref, pm01_ref, pm10_ref, pm11_ref, ds00_ref, ds01_ref, ds10_ref, ds11_ref, sum_ref,
           acc, cbuf,
           in_sem, kv_sem,
           up_s, up_r, fw_s, fw_r, pt_s, pt_r, g1_s, g1_r, g2_s, g2_r, c_s, c_r):
    i = lax.axis_index("ctx")
    dp = lax.axis_index("dp")
    n_dp = lax.axis_size("dp")
    nz, ny, nx, nc = dims
    core = lax.rem(i, nc)
    x = lax.rem(lax.div(i, nc), nx)
    ylo = lax.rem(lax.div(i, nc * nx), ny)
    z = lax.div(i, nc * nx * ny)
    partner = i + 1 - 2 * core
    spans = (i, 2 * n - 1 - i)
    rs = (core, 1 - core)
    inside = i + 2 < n
    across = jnp.where(inside, i + 2, 2 * n - 3 - i)
    has_back = i >= 2
    inside4 = i + 4 < n
    across4 = jnp.where(inside4, i + 4, 2 * n - 5 - i)
    has_back4 = i >= 4

    def dev(c, d=dp):
        return {"ctx": c, "dp": d}

    def cidx(z_, y_, x_):
        return ((z_ * ny + y_) * nx + x_) * nc + core

    def count_peers(stage):
        peers = []
        if stage == 0:
            peers.append(dev(partner))
        elif stage == 1:
            for t in range(1, nx):
                peers.append(dev(cidx(z, ylo, lax.rem(x + t, nx))))
        elif stage == 2:
            both = dp * ny + ylo
            for t in range(1, ny * n_dp):
                other = lax.rem(both + t, ny * n_dp)
                peers.append(dev(cidx(z, lax.rem(other, ny), x), lax.div(other, ny)))
        elif stage == 3:
            for t in ((1, nz - 1, nz - 2) if nz > 4 else range(1, nz)):
                peers.append(dev(cidx(lax.rem(z + t, nz), ylo, x)))
        elif nz > 4:
            peers.append(dev(cidx(lax.rem(z + 4, nz), ylo, x)))
        return peers

    def remote(src, dst, send_sem, recv_sem, target):
        return pltpu.make_async_remote_copy(src, dst, send_sem, recv_sem, device_id=target, device_id_type=MESH)

    def count_copy(stage, t, target):
        return remote(acc.at[stage], cbuf.at[stage, t], c_s.at[stage, t], c_r.at[stage, t], target)

    def count_send(stage):
        for t, target in enumerate(count_peers(stage)):
            count_copy(stage, t, target).start()

    def count_take(stage):
        total = acc[stage]
        for t, target in enumerate(count_peers(stage)):
            cp = count_copy(stage, t, target)
            cp.wait_recv()
            cp.wait_send()
            total = total + cbuf[stage, t]
        acc[stage + 1] = total

    barrier = pltpu.get_barrier_semaphore()

    def greet(target):
        pl.semaphore_signal(barrier, inc=1, device_id=target, device_id_type=MESH)

    greet(dev(across))
    pl.when(has_back)(lambda: greet(dev(i - 2)))
    n_greet = 1
    for stage in range(4):
        for target in count_peers(stage):
            greet(target)
            n_greet += 1
    if nz > 4:
        greet(dev(cidx(lax.rem(z + 2, nz), ylo, x)))
        n_greet += 1

    ins = []
    for g in range(GROUPS):
        for h in range(2):
            for w, src in enumerate((k_hbm, v_hbm)):
                cp = pltpu.make_async_copy(src.at[h, :, pl.ds(g * 128, 128)], win.at[g, h, 0, w], kv_sem.at[g, h, w])
                cp.start()
                ins.append(cp)
    cq = pltpu.make_async_copy(q_hbm, q_ref, in_sem.at[0])
    cd = pltpu.make_async_copy(do_hbm, do_ref, in_sem.at[1])
    small = [
        pltpu.make_async_copy(src, dst, in_sem.at[2 + k])
        for k, (src, dst) in enumerate(((start_hbm, start_ref), (mask_hbm, mask_ref), (seed_hbm, seed_ref)))
    ]
    for cp in small:
        cp.start()
    cq.start()
    cd.start()


    @pl.when(i < 2)
    def _():
        zeros = jnp.zeros((GROUPS, 2, SPAN, HEAD), jnp.bfloat16)
        win[:, 0, 1] = zeros
        win[:, 0, 2] = zeros
        rx2[:, 1, 0] = zeros

    @pl.when(i < 4)
    def _():
        rx2[:, 1, 1] = jnp.zeros((GROUPS, 2, SPAN, HEAD), jnp.bfloat16)

    pl.semaphore_wait(barrier, n_greet + has_back.astype(jnp.int32))

    def up_copy(g, h, forward):
        if h == 0:
            half, target = jnp.where(inside, 0, 1), dev(across)
        else:
            half, target = 1, dev(i - 2)
        sems = (fw_s, fw_r) if forward else (up_s, up_r)
        slot = 1 if forward else 0
        return remote(win.at[g, h, slot], win.at[g, half, slot + 1], sems[0].at[g, h], sems[1].at[g, half], target)

    def up_send(g, forward):
        up_copy(g, 0, forward).start()
        pl.when(has_back)(lambda: up_copy(g, 1, forward).start())

    def up_arrived(g, h, forward):
        sems = (fw_s, fw_r) if forward else (up_s, up_r)
        slot = 2 if forward else 1
        remote(win.at[g, h, slot], win.at[g, h, slot], sems[0].at[g, h], sems[1].at[g, h], dev(partner)).wait_recv()

    def partner_copy(g, h):
        return remote(win.at[g, h, pl.ds(rs[h], 2)], win.at[g, h, pl.ds(3, 2)], pt_s.at[g, h], pt_r.at[g, h], dev(partner))

    def relay(g, forward, halves=(0, 1)):
        for h in halves:
            if h == 0:
                pl.when(has_back)(lambda: up_arrived(g, 0, forward))
            else:
                up_arrived(g, 1, forward)
            if forward:
                partner_copy(g, h).start()
            elif h == 0:
                up_copy(g, 0, True).start()
            else:
                pl.when(has_back)(lambda: up_copy(g, 1, True).start())

    for g in range(GROUPS):
        for cp in ins[4 * g:4 * g + 4]:
            cp.wait()
        up_send(g, False)
    for cp in small:
        cp.wait()
    mask = mask_ref[...]
    acc[0] = jnp.pad(mask[0:1] + mask[1:2], ((0, 7), (0, 64)))
    count_send(0)
    cq.wait()
    cd.wait()

    lane = lax.broadcasted_iota(jnp.int32, (1, 128), 1)
    tri = lax.broadcasted_iota(jnp.int32, (64, 128), 0) <= (lane & 63)

    def prepare(h):
        m = mask[h:h + 1].astype(jnp.float32)
        m2 = jnp.concatenate([m, m], axis=1)
        mt_ref[h] = jnp.broadcast_to(m2, (128, 128)).T.astype(jnp.bfloat16)
        rel = relative_positions()
        start_row = start_ref[h:h + 1]
        start2 = jnp.concatenate([start_row, start_row], axis=1) - spans[h] * SPAN
        bias_ref[h] = jnp.where(rel >= start2, 0.0, MASKED)
        base = seed_ref[0] * 1000003 + spans[h] * (SPAN * 9973)
        col0 = (spans[h] * SPAN + (lane & 63)) * 40503 + base + (lane >> 6) * 7919

        def fill(pair, carry):
            keep = keep_mask(relative_positions() * 9973 + (col0 + pair * (2 * 7919)))
            keep_ref[h, pair] = jnp.where(keep, 1.0, 0.0)
            for k in range(2):
                cols = pl.ds(pl.multiple_of(pair * 256 + k * 128, 128), 128)
                do_ref[h, :, cols] = do_ref[h, :, cols] * mt_ref[h, 0:64]
            return carry

        lax.fori_loop(0, HEADS // 2, fill, 0)

    prepare(0)
    count_take(0)
    count_send(1)
    relay(0, False)
    prepare(1)
    for g in range(1, GROUPS):
        relay(g, False)
    relay(0, True)
    count_take(1)
    count_send(2)

    s_refs, d_refs = (s0_ref, s1_ref), (d0_ref, d1_ref)
    pm_refs = ((pm00_ref, pm01_ref), (pm10_ref, pm11_ref))
    ds_refs = ((ds00_ref, ds01_ref), (ds10_ref, ds11_ref))

    def kv_here(g, h):
        partner_copy(g, h).wait_recv()

    def stack(ref, g, h, hh):
        return jnp.concatenate(
            [ref[h, :, pl.ds(pl.multiple_of(g * 1024 + (hh * 4 + j) * 128, 128), 128)] for j in range(4)], axis=0)

    def scores(g, h, hh, which=(0, 1)):
        if 0 in which:
            s_refs[hh][...] = nt(win[g, h, :, 0].reshape(320, 128), stack(q_ref, g, h, hh))
        if 1 in which:
            d_refs[hh][...] = nt(win[g, h, :, 1].reshape(320, 128), stack(do_ref, g, h, hh))

    def soft(g, h, hh, prs=(0, 1)):
        s_ref, d_ref = s_refs[hh], d_refs[hh]
        for pr in prs:
            cs = slice(pr * 128, pr * 128 + 128)
            s = jnp.concatenate([s_ref[64:128, cs], s_ref[192:320, cs], jnp.where(tri, s_ref[0:64, cs], s_ref[128:192, cs])], axis=0)
            s = s + bias_ref[h]
            top = jnp.max(s, axis=0, keepdims=True)
            e = jnp.exp2((s - top) * EXP2_SCALE)
            p = e * (1.0 / jnp.sum(e, axis=0, keepdims=True))
            pm = p * keep_ref[h, g * 4 + hh * 2 + pr]
            dpv = jnp.concatenate([d_ref[64:128, cs], d_ref[192:320, cs], jnp.where(tri, d_ref[0:64, cs], d_ref[128:192, cs])], axis=0)
            t = pm * dpv
            ds = t - p * jnp.sum(t, axis=0, keepdims=True)
            for ref, val in ((pm_refs[h][hh], pm), (ds_refs[h][hh], ds)):
                ref[g, 0:64, cs] = jnp.where(tri, val[192:], 0.0).astype(jnp.bfloat16)
                ref[g, 64:128, cs] = val[:64].astype(jnp.bfloat16)
                ref[g, 128:192, cs] = jnp.where(tri, 0.0, val[192:]).astype(jnp.bfloat16)
                ref[g, 192:320, cs] = val[64:192].astype(jnp.bfloat16)

    def products(g, h, hh):
        for w, (ref, other) in enumerate(((ds_refs[h][hh], q_ref), (pm_refs[h][hh], do_ref))):
            val = nn(ref[g], stack(other, g, h, hh))
            if hh == 0:
                sum_ref[w] = val
            else:
                val = val + sum_ref[w]
                own[g, h, w] = val[0:64]
                part[g, h, :, w] = val.reshape(5, SPAN, HEAD).astype(jnp.bfloat16)

    def outputs(g, h):
        kt = win[g, h, :, 0].reshape(320, 128).T
        vt = win[g, h, :, 1].reshape(320, 128).T
        for hh in range(2):
            oo = (nn(vt, pm_refs[h][hh][g]) * KEEP_SCALE).astype(jnp.bfloat16).T
            dq = nn(kt, ds_refs[h][hh][g]).astype(jnp.bfloat16).T
            for j in range(4):
                cols = pl.ds(pl.multiple_of(g * 1024 + (hh * 4 + j) * 128, 128), 128)
                o_ref[h, :, cols] = oo[j * 64:(j + 1) * 64]
                dqo_ref[h, :, cols] = dq[j * 64:(j + 1) * 64]

    def block(sc, so, pr):
        products(*pr)
        soft(*so)
        scores(*sc)

    def grad1_copy(g, h):
        return remote(part.at[g, h, pl.ds(3, 2)], rx1.at[g, h], g1_s.at[g, h], g1_r.at[g, h], dev(partner))

    def share(g, h):
        grad1_copy(g, h).start()

    def down_copy(g, h, e):
        if h == 0:
            half, target = 0, dev(i - 2 - 2 * e)
        else:
            half = jnp.where((inside, inside4)[e], 1, 0)
            target = dev((across, across4)[e])
        return remote(tot.at[g, h, e], rx2.at[g, half, e], g2_s.at[g, h, e], g2_r.at[g, half, e], target)

    def down_arrived(g, h, e):
        def take():
            remote(rx2.at[g, h, e], rx2.at[g, h, e], g2_s.at[g, h, e], g2_r.at[g, h, e], dev(partner)).wait_recv()

        if h == 0:
            take()
        else:
            pl.when((has_back, has_back4)[e])(take)

    def combine(g, h):
        r = rs[h]
        grad1_copy(g, h).wait_recv()
        tot[g, h, 1] = part[g, h, 2] + rx1[g, h, 1] * r.astype(jnp.bfloat16)
        tot[g, h, 0] = part[g, h, 1] + rx1[g, h, 1 - r]
        for e in (1, 0):
            if h == 0:
                pl.when((has_back, has_back4)[e])(lambda e=e: down_copy(g, h, e).start())
            else:
                down_copy(g, h, e).start()

    kv_here(0, 0)
    scores(0, 0, 0)
    pm11_ref[0] = jnp.zeros((320, 256), jnp.bfloat16)
    ds11_ref[0] = jnp.zeros((320, 256), jnp.bfloat16)

    def step(g, carry):
        before = jnp.maximum(g - 1, 0)
        after = jnp.minimum(g + 1, GROUPS - 1)
        pl.when(g < GROUPS - 1)(lambda: relay(g + 1, True))
        block((g, 0, 1), (g, 0, 0), (before, 1, 1))

        @pl.when(g > 0)
        def _():
            share(g - 1, 1)

        kv_here(g, 1)
        block((g, 1, 0), (g, 0, 1), (g, 0, 0))
        block((g, 1, 1), (g, 1, 0), (g, 0, 1))
        share(g, 0)
        pl.when(g > 0)(lambda: combine(g - 1, 0))

        @pl.when(g == 1)
        def _():
            count_take(2)
            count_send(3)

        @pl.when(g == 3)
        def _():
            count_take(3)
            count_send(4)

        pl.when(g < GROUPS - 1)(lambda: kv_here(g + 1, 0))
        block((after, 0, 0), (g, 1, 1), (g, 1, 0))
        pl.when(g > 0)(lambda: combine(g - 1, 1))
        return carry

    lax.fori_loop(0, GROUPS, step, 0)
    products(GROUPS - 1, 1, 1)
    share(GROUPS - 1, 1)
    combine(GROUPS - 1, 0)
    def finish(g, carry):
        for h in range(2):
            outputs(g, h)
        return carry

    finish(0, 0)
    combine(GROUPS - 1, 1)
    lax.fori_loop(1, GROUPS, finish, 0)

    def drain(g, carry):
        for h in range(2):
            partner_copy(g, h).wait_send()
            grad1_copy(g, h).wait_send()
            down_copy(g, 1, h).wait_send()
            pl.when((has_back, has_back4)[h])(lambda h=h: down_copy(g, 0, h).wait_send())
        for flag in (False, True):
            up_copy(g, 0, flag).wait_send()
            pl.when(has_back)(lambda flag=flag: up_copy(g, 1, flag).wait_send())
        return carry

    lax.fori_loop(0, GROUPS, drain, 0)

    def arrived(g):
        for h in range(2):
            for e in range(2):
                down_arrived(g, h, e)

    for g in range(GROUPS - 1):
        arrived(g)
    count_take(4)
    total = jnp.sum(acc[5].astype(jnp.float32))
    slots = float(2 * 2 * n * SPAN)
    factor = jnp.full((1, 128), slots * KEEP_SCALE, jnp.float32) / jnp.full((1, 128), total, jnp.float32)

    def rescale(g, carry):
        for h in range(2):
            for j in range(8):
                cols = pl.ds(pl.multiple_of(g * 1024 + j * 128, 128), 128)
                dqo_ref[h, :, cols] = (dqo_ref[h, :, cols].astype(jnp.float32) * (factor * INV)).astype(jnp.bfloat16)
        return carry

    def final(g, carry):
        for h in range(2):
            val = own[g, h] + (1 - rs[h]).astype(jnp.float32) * rx1[g, h, 0].astype(jnp.float32)
            val = val + rx2[g, h, 0].astype(jnp.float32) + rx2[g, h, 1].astype(jnp.float32)
            cols = pl.ds(pl.multiple_of(g * 128, 128), 128)
            dkv_ref[0, h, :, cols] = val[0] * (factor * INV)
            dkv_ref[1, h, :, cols] = val[1] * factor
        return carry

    lax.fori_loop(0, GROUPS, rescale, 0)
    lax.fori_loop(0, GROUPS - 1, final, 0)
    arrived(GROUPS - 1)
    final(GROUPS - 1, 0)


def store_kernel(o_ref, dq_ref, dkv_ref, o_hbm, dq_hbm, dk_hbm, dv_hbm, sems):
    copies = [
        pltpu.make_async_copy(o_ref, o_hbm, sems.at[0]),
        pltpu.make_async_copy(dq_ref, dq_hbm, sems.at[1]),
        pltpu.make_async_copy(dkv_ref.at[0], dk_hbm, sems.at[2]),
        pltpu.make_async_copy(dkv_ref.at[1], dv_hbm, sems.at[3]),
    ]
    for cp in copies:
        cp.start()
    for cp in copies:
        cp.wait()


def grid_of(n):
    nc, nx = 2, 4
    ny = 2 if n // (nc * nx) > 1 else 1
    return (n // (nc * nx * ny), ny, nx, nc)


def body(queries, keys, values, cotangent, doc_start, loss_mask, seeds):
    n = lax.axis_size("ctx")
    dims = grid_of(n)
    peers = max(1, dims[2] - 1, dims[1] * lax.axis_size("dp") - 1, dims[0] - 1)
    wide = (2, SPAN, HEADS * HEAD)
    narrow = (2, SPAN, GROUPS * HEAD)
    bf16, f32, i32 = jnp.bfloat16, jnp.float32, jnp.int32
    hbm = pl.BlockSpec(memory_space=pl.ANY)
    vmem = pl.BlockSpec(memory_space=pltpu.VMEM)
    dma = pltpu.SemaphoreType.DMA
    pair = (2, SPAN, HEAD)
    held = pl.pallas_call(
        functools.partial(kernel, n, dims),
        out_shape=[pltpu.VMEM(wide, bf16), pltpu.VMEM(wide, bf16), pltpu.VMEM((2,) + narrow, f32)],
        in_specs=[hbm] * 7,
        out_specs=[vmem] * 3,
        scratch_shapes=[
            pltpu.VMEM(wide, bf16),
            pltpu.VMEM(wide, bf16),
            pltpu.VMEM((2, SPAN), i32),
            pltpu.VMEM((2, SPAN), i32),
            pltpu.SMEM((1,), i32),
            pltpu.VMEM((GROUPS, 2, 5) + pair, bf16),
            pltpu.VMEM((GROUPS, 2, 5) + pair, bf16),
            pltpu.VMEM((GROUPS, 2) + pair, f32),
            pltpu.VMEM((GROUPS, 2, 2) + pair, bf16),
            pltpu.VMEM((GROUPS, 2, 2) + pair, bf16),
            pltpu.VMEM((GROUPS, 2, 2) + pair, bf16),
            pltpu.VMEM((2, HEADS // 2, 256, 128), f32),
            pltpu.VMEM((2, 256, 128), f32),
            pltpu.VMEM((2, 128, 128), bf16),
        ] + [pltpu.VMEM((320, 256), f32)] * 4 + [pltpu.VMEM((GROUPS, 320, 256), bf16)] * 8 + [
            pltpu.VMEM((2, 320, 128), f32),
            pltpu.VMEM((6, 8, 128), i32),
            pltpu.VMEM((5, peers, 8, 128), i32),
            dma((5,)),
            dma((GROUPS, 2, 2)),
        ] + [dma((GROUPS, 2))] * 8 + [dma((GROUPS, 2, 2))] * 2 + [dma((5, peers))] * 2,
        compiler_params=pltpu.CompilerParams(collective_id=0, has_side_effects=True),
        name="attention",
    )(
        queries.reshape(wide),
        cotangent.reshape(wide),
        keys.reshape(narrow),
        values.reshape(narrow),
        doc_start.reshape(2, SPAN),
        loss_mask.reshape(2, SPAN),
        seeds,
    )
    outs = pl.pallas_call(
        store_kernel,
        out_shape=[
            jax.ShapeDtypeStruct(wide, bf16),
            jax.ShapeDtypeStruct(wide, bf16),
            jax.ShapeDtypeStruct(narrow, f32),
            jax.ShapeDtypeStruct(narrow, f32),
        ],
        in_specs=[vmem] * 3,
        out_specs=[hbm] * 4,
        scratch_shapes=[dma((4,))],
        name="store",
    )(*[pltpu.with_memory_space_constraint(x, pltpu.VMEM) for x in held])
    return (
        outs[0].reshape(queries.shape),
        outs[1].reshape(queries.shape),
        outs[2].reshape(keys.shape),
        outs[3].reshape(values.shape),
    )


def solution(mesh):
    wide = P("dp", None, "ctx", None, None)
    flat = P("dp", None, "ctx", None)
    return jax.shard_map(
        body,
        mesh=mesh,
        in_specs=(wide, wide, wide, wide, flat, flat, P("dp")),
        out_specs=(wide, wide, wide, wide),
        check_vma=False,
    )
```

```python
import functools
import math

import jax
import jax.numpy as jnp
from jax import lax
from jax.experimental import pallas as pl
from jax.experimental.pallas import tpu as pltpu
from jax.sharding import PartitionSpec as P

SPAN = 64
GROUPS = 4
HEADS = 32
HEAD = 128
INV = 1.0 / math.sqrt(HEAD)
KEEP_SCALE = 1024.0 / 922.0
EXP2_SCALE = INV * math.log2(math.e)
MASKED = -1e30
MESH = pl.DeviceIdType.MESH


def nt(a, b):
    return lax.dot_general(a, b, (((1,), (1,)), ((), ())), preferred_element_type=jnp.float32)


def nn(a, b):
    return lax.dot_general(a, b, (((1,), (0,)), ((), ())), preferred_element_type=jnp.float32)


def keep_mask(mixed):
    mixed = mixed ^ lax.shift_right_arithmetic(mixed, 15)
    mixed = mixed * 73244475
    mixed = mixed ^ lax.shift_right_arithmetic(mixed, 13)
    mixed = mixed * 1274126177
    mixed = mixed ^ lax.shift_right_arithmetic(mixed, 16)
    return (mixed & 1023) >= 102


def relative_positions():
    row = lax.broadcasted_iota(jnp.int32, (256, 128), 0)
    offset = lax.broadcasted_iota(jnp.int32, (256, 128), 1) & 63
    tile = row >> 6
    inner = row & 63
    apart = jnp.where(tile == 0, 2, jnp.where(tile == 1, 1, 3))
    behind = jnp.where(tile == 3, jnp.where(inner <= offset, 0, 4), apart)
    return inner - 64 * behind


def kernel(n, dims, q_hbm, do_hbm, k_hbm, v_hbm, start_hbm, mask_hbm, seed_hbm,
           o_ref, dqo_ref, dkv_ref,
           q_ref, do_ref, start_ref, mask_ref, seed_ref,
           win, part, own, rx1, tot, rx2, keep_ref, bias_ref, mt_ref,
           s0_ref, s1_ref, d0_ref, d1_ref, pm00_ref, pm01_ref, pm10_ref, pm11_ref, ds00_ref, ds01_ref, ds10_ref, ds11_ref, sum_ref,
           acc, cbuf,
           in_sem, kv_sem,
           up_s, up_r, fw_s, fw_r, pt_s, pt_r, g1_s, g1_r, g2_s, g2_r, c_s, c_r):
    i = lax.axis_index("ctx")
    dp = lax.axis_index("dp")
    n_dp = lax.axis_size("dp")
    nz, ny, nx, nc = dims
    core = lax.rem(i, nc)
    x = lax.rem(lax.div(i, nc), nx)
    ylo = lax.rem(lax.div(i, nc * nx), ny)
    z = lax.div(i, nc * nx * ny)
    partner = i + 1 - 2 * core
    spans = (i, 2 * n - 1 - i)
    rs = (core, 1 - core)
    inside = i + 2 < n
    across = jnp.where(inside, i + 2, 2 * n - 3 - i)
    has_back = i >= 2
    inside4 = i + 4 < n
    across4 = jnp.where(inside4, i + 4, 2 * n - 5 - i)
    has_back4 = i >= 4

    def dev(c, d=dp):
        return {"ctx": c, "dp": d}

    def cidx(z_, y_, x_):
        return ((z_ * ny + y_) * nx + x_) * nc + core

    def count_peers(stage):
        peers = []
        if stage == 0:
            peers.append(dev(partner))
        elif stage == 1:
            for t in range(1, nx):
                peers.append(dev(cidx(z, ylo, lax.rem(x + t, nx))))
        elif stage == 2:
            both = dp * ny + ylo
            for t in range(1, ny * n_dp):
                other = lax.rem(both + t, ny * n_dp)
                peers.append(dev(cidx(z, lax.rem(other, ny), x), lax.div(other, ny)))
        elif stage == 3:
            for t in ((1, nz - 1, nz - 2) if nz > 4 else range(1, nz)):
                peers.append(dev(cidx(lax.rem(z + t, nz), ylo, x)))
        elif nz > 4:
            peers.append(dev(cidx(lax.rem(z + 4, nz), ylo, x)))
        return peers

    def remote(src, dst, send_sem, recv_sem, target):
        return pltpu.make_async_remote_copy(src, dst, send_sem, recv_sem, device_id=target, device_id_type=MESH)

    def count_copy(stage, t, target):
        return remote(acc.at[stage], cbuf.at[stage, t], c_s.at[stage, t], c_r.at[stage, t], target)

    def count_send(stage):
        for t, target in enumerate(count_peers(stage)):
            count_copy(stage, t, target).start()

    def count_take(stage):
        total = acc[stage]
        for t, target in enumerate(count_peers(stage)):
            cp = count_copy(stage, t, target)
            cp.wait_recv()
            cp.wait_send()
            total = total + cbuf[stage, t]
        acc[stage + 1] = total

    barrier = pltpu.get_barrier_semaphore()

    def greet(target):
        pl.semaphore_signal(barrier, inc=1, device_id=target, device_id_type=MESH)

    greet(dev(across))
    pl.when(has_back)(lambda: greet(dev(i - 2)))
    n_greet = 1
    for stage in range(4):
        for target in count_peers(stage):
            greet(target)
            n_greet += 1
    if nz > 4:
        greet(dev(cidx(lax.rem(z + 2, nz), ylo, x)))
        n_greet += 1

    ins = []
    for g in range(GROUPS):
        for h in range(2):
            for w, src in enumerate((k_hbm, v_hbm)):
                cp = pltpu.make_async_copy(src.at[h, :, pl.ds(g * 128, 128)], win.at[g, h, 0, w], kv_sem.at[g, h, w])
                cp.start()
                ins.append(cp)
    cq = pltpu.make_async_copy(q_hbm, q_ref, in_sem.at[0])
    cd = pltpu.make_async_copy(do_hbm, do_ref, in_sem.at[1])
    small = [
        pltpu.make_async_copy(src, dst, in_sem.at[2 + k])
        for k, (src, dst) in enumerate(((start_hbm, start_ref), (mask_hbm, mask_ref), (seed_hbm, seed_ref)))
    ]
    for cp in small:
        cp.start()
    cq.start()
    cd.start()


    @pl.when(i < 2)
    def _():
        zeros = jnp.zeros((GROUPS, 2, SPAN, HEAD), jnp.bfloat16)
        win[:, 0, 1] = zeros
        win[:, 0, 2] = zeros
        rx2[:, 1, 0] = zeros

    @pl.when(i < 4)
    def _():
        rx2[:, 1, 1] = jnp.zeros((GROUPS, 2, SPAN, HEAD), jnp.bfloat16)

    pl.semaphore_wait(barrier, n_greet + has_back.astype(jnp.int32))

    def up_copy(g, h, forward):
        if h == 0:
            half, target = jnp.where(inside, 0, 1), dev(across)
        else:
            half, target = 1, dev(i - 2)
        sems = (fw_s, fw_r) if forward else (up_s, up_r)
        slot = 1 if forward else 0
        return remote(win.at[g, h, slot], win.at[g, half, slot + 1], sems[0].at[g, h], sems[1].at[g, half], target)

    def up_send(g, forward):
        up_copy(g, 0, forward).start()
        pl.when(has_back)(lambda: up_copy(g, 1, forward).start())

    def up_arrived(g, h, forward):
        sems = (fw_s, fw_r) if forward else (up_s, up_r)
        slot = 2 if forward else 1
        remote(win.at[g, h, slot], win.at[g, h, slot], sems[0].at[g, h], sems[1].at[g, h], dev(partner)).wait_recv()

    def partner_copy(g, h):
        return remote(win.at[g, h, pl.ds(rs[h], 2)], win.at[g, h, pl.ds(3, 2)], pt_s.at[g, h], pt_r.at[g, h], dev(partner))

    def relay(g, forward, halves=(0, 1)):
        for h in halves:
            if h == 0:
                pl.when(has_back)(lambda: up_arrived(g, 0, forward))
            else:
                up_arrived(g, 1, forward)
            if forward:
                partner_copy(g, h).start()
            elif h == 0:
                up_copy(g, 0, True).start()
            else:
                pl.when(has_back)(lambda: up_copy(g, 1, True).start())

    for g in range(GROUPS):
        for cp in ins[4 * g:4 * g + 4]:
            cp.wait()
        up_send(g, False)
    for cp in small:
        cp.wait()
    mask = mask_ref[...]
    acc[0] = jnp.pad(mask[0:1] + mask[1:2], ((0, 7), (0, 64)))
    count_send(0)
    cq.wait()
    cd.wait()

    lane = lax.broadcasted_iota(jnp.int32, (1, 128), 1)
    tri = lax.broadcasted_iota(jnp.int32, (64, 128), 0) <= (lane & 63)

    def prepare(h):
        m = mask[h:h + 1].astype(jnp.float32)
        m2 = jnp.concatenate([m, m], axis=1)
        mt_ref[h] = jnp.broadcast_to(m2, (128, 128)).T.astype(jnp.bfloat16)
        rel = relative_positions()
        start_row = start_ref[h:h + 1]
        start2 = jnp.concatenate([start_row, start_row], axis=1) - spans[h] * SPAN
        bias_ref[h] = jnp.where(rel >= start2, 0.0, MASKED)
        base = seed_ref[0] * 1000003 + spans[h] * (SPAN * 9973)
        col0 = (spans[h] * SPAN + (lane & 63)) * 40503 + base + (lane >> 6) * 7919

        def fill(pair, carry):
            keep = keep_mask(relative_positions() * 9973 + (col0 + pair * (2 * 7919)))
            keep_ref[h, pair] = jnp.where(keep, 1.0, 0.0)
            for k in range(2):
                cols = pl.ds(pl.multiple_of(pair * 256 + k * 128, 128), 128)
                do_ref[h, :, cols] = do_ref[h, :, cols] * mt_ref[h, 0:64]
            return carry

        lax.fori_loop(0, HEADS // 2, fill, 0)

    prepare(0)
    count_take(0)
    count_send(1)
    relay(0, False)
    relay(1, False)
    prepare(1)
    for g in range(2, GROUPS):
        relay(g, False)
    relay(0, True)
    count_take(1)
    count_send(2)

    s_refs, d_refs = (s0_ref, s1_ref), (d0_ref, d1_ref)
    pm_refs = ((pm00_ref, pm01_ref), (pm10_ref, pm11_ref))
    ds_refs = ((ds00_ref, ds01_ref), (ds10_ref, ds11_ref))

    def kv_here(g, h):
        partner_copy(g, h).wait_recv()

    def stack(ref, g, h, hh):
        return jnp.concatenate(
            [ref[h, :, pl.ds(pl.multiple_of(g * 1024 + (hh * 4 + j) * 128, 128), 128)] for j in range(4)], axis=0)

    def scores(g, h, hh, which=(0, 1)):
        if 0 in which:
            s_refs[hh][...] = nt(win[g, h, :, 0].reshape(320, 128), stack(q_ref, g, h, hh))
        if 1 in which:
            d_refs[hh][...] = nt(win[g, h, :, 1].reshape(320, 128), stack(do_ref, g, h, hh))

    def soft(g, h, hh, prs=(0, 1)):
        s_ref, d_ref = s_refs[hh], d_refs[hh]
        for pr in prs:
            cs = slice(pr * 128, pr * 128 + 128)
            s = jnp.concatenate([s_ref[64:128, cs], s_ref[192:320, cs], jnp.where(tri, s_ref[0:64, cs], s_ref[128:192, cs])], axis=0)
            s = s + bias_ref[h]
            top = jnp.max(s, axis=0, keepdims=True)
            e = jnp.exp2((s - top) * EXP2_SCALE)
            p = e * (1.0 / jnp.sum(e, axis=0, keepdims=True))
            pm = p * keep_ref[h, g * 4 + hh * 2 + pr]
            dpv = jnp.concatenate([d_ref[64:128, cs], d_ref[192:320, cs], jnp.where(tri, d_ref[0:64, cs], d_ref[128:192, cs])], axis=0)
            t = pm * dpv
            ds = t - p * jnp.sum(t, axis=0, keepdims=True)
            for ref, val in ((pm_refs[h][hh], pm), (ds_refs[h][hh], ds)):
                ref[g, 0:64, cs] = jnp.where(tri, val[192:], 0.0).astype(jnp.bfloat16)
                ref[g, 64:128, cs] = val[:64].astype(jnp.bfloat16)
                ref[g, 128:192, cs] = jnp.where(tri, 0.0, val[192:]).astype(jnp.bfloat16)
                ref[g, 192:320, cs] = val[64:192].astype(jnp.bfloat16)

    def products(g, h, hh):
        for w, (ref, other) in enumerate(((ds_refs[h][hh], q_ref), (pm_refs[h][hh], do_ref))):
            val = nn(ref[g], stack(other, g, h, hh))
            if hh == 0:
                sum_ref[w] = val
            else:
                val = val + sum_ref[w]
                own[g, h, w] = val[0:64]
                part[g, h, :, w] = val.reshape(5, SPAN, HEAD).astype(jnp.bfloat16)

    def outputs(g, h):
        kt = win[g, h, :, 0].reshape(320, 128).T
        vt = win[g, h, :, 1].reshape(320, 128).T
        for hh in range(2):
            oo = (nn(vt, pm_refs[h][hh][g]) * KEEP_SCALE).astype(jnp.bfloat16).T
            dq = nn(kt, ds_refs[h][hh][g]).astype(jnp.bfloat16).T
            for j in range(4):
                cols = pl.ds(pl.multiple_of(g * 1024 + (hh * 4 + j) * 128, 128), 128)
                o_ref[h, :, cols] = oo[j * 64:(j + 1) * 64]
                dqo_ref[h, :, cols] = dq[j * 64:(j + 1) * 64]

    def block(sc, so, pr):
        products(*pr)
        soft(*so)
        scores(*sc)

    def grad1_copy(g, h):
        return remote(part.at[g, h, pl.ds(3, 2)], rx1.at[g, h], g1_s.at[g, h], g1_r.at[g, h], dev(partner))

    def share(g, h):
        grad1_copy(g, h).start()

    def down_copy(g, h, e):
        if h == 0:
            half, target = 0, dev(i - 2 - 2 * e)
        else:
            half = jnp.where((inside, inside4)[e], 1, 0)
            target = dev((across, across4)[e])
        return remote(tot.at[g, h, e], rx2.at[g, half, e], g2_s.at[g, h, e], g2_r.at[g, half, e], target)

    def down_arrived(g, h, e):
        def take():
            remote(rx2.at[g, h, e], rx2.at[g, h, e], g2_s.at[g, h, e], g2_r.at[g, h, e], dev(partner)).wait_recv()

        if h == 0:
            take()
        else:
            pl.when((has_back, has_back4)[e])(take)

    def combine(g, h):
        r = rs[h]
        grad1_copy(g, h).wait_recv()
        tot[g, h, 1] = part[g, h, 2] + rx1[g, h, 1] * r.astype(jnp.bfloat16)
        tot[g, h, 0] = part[g, h, 1] + rx1[g, h, 1 - r]
        for e in (1, 0):
            if h == 0:
                pl.when((has_back, has_back4)[e])(lambda e=e: down_copy(g, h, e).start())
            else:
                down_copy(g, h, e).start()

    kv_here(0, 0)
    scores(0, 0, 0)
    pm11_ref[0] = jnp.zeros((320, 256), jnp.bfloat16)
    ds11_ref[0] = jnp.zeros((320, 256), jnp.bfloat16)

    def step(g, carry):
        before = jnp.maximum(g - 1, 0)
        after = jnp.minimum(g + 1, GROUPS - 1)
        pl.when(g < GROUPS - 1)(lambda: relay(g + 1, True))
        block((g, 0, 1), (g, 0, 0), (before, 1, 1))

        @pl.when(g > 0)
        def _():
            share(g - 1, 1)

        kv_here(g, 1)
        block((g, 1, 0), (g, 0, 1), (g, 0, 0))
        block((g, 1, 1), (g, 1, 0), (g, 0, 1))
        share(g, 0)
        pl.when(g > 0)(lambda: combine(g - 1, 0))

        @pl.when(g == 1)
        def _():
            count_take(2)
            count_send(3)

        @pl.when(g == 3)
        def _():
            count_take(3)
            count_send(4)

        pl.when(g < GROUPS - 1)(lambda: kv_here(g + 1, 0))
        block((after, 0, 0), (g, 1, 1), (g, 1, 0))
        pl.when(g > 0)(lambda: combine(g - 1, 1))
        return carry

    lax.fori_loop(0, GROUPS, step, 0)
    products(GROUPS - 1, 1, 1)
    share(GROUPS - 1, 1)
    combine(GROUPS - 1, 0)
    def finish(g, carry):
        for h in range(2):
            outputs(g, h)
        return carry

    finish(0, 0)
    combine(GROUPS - 1, 1)
    lax.fori_loop(1, GROUPS, finish, 0)

    def drain(g, carry):
        for h in range(2):
            partner_copy(g, h).wait_send()
            grad1_copy(g, h).wait_send()
            down_copy(g, 1, h).wait_send()
            pl.when((has_back, has_back4)[h])(lambda h=h: down_copy(g, 0, h).wait_send())
        for flag in (False, True):
            up_copy(g, 0, flag).wait_send()
            pl.when(has_back)(lambda flag=flag: up_copy(g, 1, flag).wait_send())
        return carry

    lax.fori_loop(0, GROUPS, drain, 0)

    def arrived(g):
        for h in range(2):
            for e in range(2):
                down_arrived(g, h, e)

    for g in range(GROUPS - 1):
        arrived(g)
    count_take(4)
    total = jnp.sum(acc[5].astype(jnp.float32))
    slots = float(2 * 2 * n * SPAN)
    factor = jnp.full((1, 128), slots * KEEP_SCALE, jnp.float32) / jnp.full((1, 128), total, jnp.float32)

    def rescale(g, carry):
        for h in range(2):
            for j in range(8):
                cols = pl.ds(pl.multiple_of(g * 1024 + j * 128, 128), 128)
                dqo_ref[h, :, cols] = (dqo_ref[h, :, cols].astype(jnp.float32) * (factor * INV)).astype(jnp.bfloat16)
        return carry

    def final(g, carry):
        for h in range(2):
            val = own[g, h] + (1 - rs[h]).astype(jnp.float32) * rx1[g, h, 0].astype(jnp.float32)
            val = val + rx2[g, h, 0].astype(jnp.float32) + rx2[g, h, 1].astype(jnp.float32)
            cols = pl.ds(pl.multiple_of(g * 128, 128), 128)
            dkv_ref[0, h, :, cols] = val[0] * (factor * INV)
            dkv_ref[1, h, :, cols] = val[1] * factor
        return carry

    lax.fori_loop(0, GROUPS, rescale, 0)
    lax.fori_loop(0, GROUPS - 1, final, 0)
    arrived(GROUPS - 1)
    final(GROUPS - 1, 0)


def store_kernel(o_ref, dq_ref, dkv_ref, o_hbm, dq_hbm, dk_hbm, dv_hbm, sems):
    copies = [
        pltpu.make_async_copy(o_ref, o_hbm, sems.at[0]),
        pltpu.make_async_copy(dq_ref, dq_hbm, sems.at[1]),
        pltpu.make_async_copy(dkv_ref.at[0], dk_hbm, sems.at[2]),
        pltpu.make_async_copy(dkv_ref.at[1], dv_hbm, sems.at[3]),
    ]
    for cp in copies:
        cp.start()
    for cp in copies:
        cp.wait()


def grid_of(n):
    nc, nx = 2, 4
    ny = 2 if n // (nc * nx) > 1 else 1
    return (n // (nc * nx * ny), ny, nx, nc)


def body(queries, keys, values, cotangent, doc_start, loss_mask, seeds):
    n = lax.axis_size("ctx")
    dims = grid_of(n)
    peers = max(1, dims[2] - 1, dims[1] * lax.axis_size("dp") - 1, dims[0] - 1)
    wide = (2, SPAN, HEADS * HEAD)
    narrow = (2, SPAN, GROUPS * HEAD)
    bf16, f32, i32 = jnp.bfloat16, jnp.float32, jnp.int32
    hbm = pl.BlockSpec(memory_space=pl.ANY)
    vmem = pl.BlockSpec(memory_space=pltpu.VMEM)
    dma = pltpu.SemaphoreType.DMA
    pair = (2, SPAN, HEAD)
    held = pl.pallas_call(
        functools.partial(kernel, n, dims),
        out_shape=[pltpu.VMEM(wide, bf16), pltpu.VMEM(wide, bf16), pltpu.VMEM((2,) + narrow, f32)],
        in_specs=[hbm] * 7,
        out_specs=[vmem] * 3,
        scratch_shapes=[
            pltpu.VMEM(wide, bf16),
            pltpu.VMEM(wide, bf16),
            pltpu.VMEM((2, SPAN), i32),
            pltpu.VMEM((2, SPAN), i32),
            pltpu.SMEM((1,), i32),
            pltpu.VMEM((GROUPS, 2, 5) + pair, bf16),
            pltpu.VMEM((GROUPS, 2, 5) + pair, bf16),
            pltpu.VMEM((GROUPS, 2) + pair, f32),
            pltpu.VMEM((GROUPS, 2, 2) + pair, bf16),
            pltpu.VMEM((GROUPS, 2, 2) + pair, bf16),
            pltpu.VMEM((GROUPS, 2, 2) + pair, bf16),
            pltpu.VMEM((2, HEADS // 2, 256, 128), f32),
            pltpu.VMEM((2, 256, 128), f32),
            pltpu.VMEM((2, 128, 128), bf16),
        ] + [pltpu.VMEM((320, 256), f32)] * 4 + [pltpu.VMEM((GROUPS, 320, 256), bf16)] * 8 + [
            pltpu.VMEM((2, 320, 128), f32),
            pltpu.VMEM((6, 8, 128), i32),
            pltpu.VMEM((5, peers, 8, 128), i32),
            dma((5,)),
            dma((GROUPS, 2, 2)),
        ] + [dma((GROUPS, 2))] * 8 + [dma((GROUPS, 2, 2))] * 2 + [dma((5, peers))] * 2,
        compiler_params=pltpu.CompilerParams(collective_id=0, has_side_effects=True),
        name="attention",
    )(
        queries.reshape(wide),
        cotangent.reshape(wide),
        keys.reshape(narrow),
        values.reshape(narrow),
        doc_start.reshape(2, SPAN),
        loss_mask.reshape(2, SPAN),
        seeds,
    )
    outs = pl.pallas_call(
        store_kernel,
        out_shape=[
            jax.ShapeDtypeStruct(wide, bf16),
            jax.ShapeDtypeStruct(wide, bf16),
            jax.ShapeDtypeStruct(narrow, f32),
            jax.ShapeDtypeStruct(narrow, f32),
        ],
        in_specs=[vmem] * 3,
        out_specs=[hbm] * 4,
        scratch_shapes=[dma((4,))],
        name="store",
    )(*[pltpu.with_memory_space_constraint(x, pltpu.VMEM) for x in held])
    return (
        outs[0].reshape(queries.shape),
        outs[1].reshape(queries.shape),
        outs[2].reshape(keys.shape),
        outs[3].reshape(values.shape),
    )


def solution(mesh):
    wide = P("dp", None, "ctx", None, None)
    flat = P("dp", None, "ctx", None)
    return jax.shard_map(
        body,
        mesh=mesh,
        in_specs=(wide, wide, wide, wide, flat, flat, P("dp")),
        out_specs=(wide, wide, wide, wide),
        check_vma=False,
    )
```
